256 devices in a mesh: rows: 64 (over y, x_hi, z), heads: 4 (over x_lo, core).
Axes of the slice: x: 4 (x_hi: 2, x_lo: 2; x = x_hi * 2 + x_lo), y: 4, z: 8, core: 2. Of those that a mesh axis runs over, the one named last changes fastest.
Arguments:
- tokens: bfloat16 [256, 512, 768], P('rows', None, 'heads'), may hold values from -24 to 24
- qkv_weight: bfloat16 [2, 768, 3, 768], replicated, may hold values from -0.21875 to 0.21875
- out_weight: bfloat16 [2, 768, 768], replicated, may hold values from -0.21875 to 0.21875
- norm_gain: bfloat16 [2, 768], replicated, may hold values from 0.099609375 to 1.8984375
Outputs:
- stream: bfloat16 [256, 512, 768], P('rows', None, 'heads')
The draws below stay inside these ranges and needn't reach their ends.
All inputs are finite; a program needn't handle non-finite values.
Results may differ from the reference program's by a relative error of at most 0.0096.
Values may be sent and summed in bfloat16 or wider, within the bound.
A program may use at most 64 MiB of HBM per device.

```python
import jax
import jax.numpy as jnp
from jax import lax

D = 768
HEADS = 12
HEAD_DIM = 64
RESIDUES = 512
LAYERS = 2
BLOCKS = 2
SEQS = 256


def draw_tokens(key, part):
    entries = jnp.clip(jax.random.normal(key, (SEQS, RESIDUES, D), jnp.float32), -6.0, 6.0)
    return entries.astype(jnp.bfloat16)


def gaussian(own_key, extent, deviation, bound, held_as=jnp.bfloat16):
    drawn = deviation * jax.random.normal(own_key, extent, jnp.float32)
    return jnp.clip(drawn, min=-bound, max=bound).astype(held_as)


def setup_inputs(seed: int = 0) -> dict:
    key_list = jax.random.split(jax.random.key(seed), 5)
    return {
        "tokens": draw_tokens(jax.random.fold_in(key_list[4], 71), 0),
        "qkv_weight": gaussian(key_list[1], (LAYERS, D, 3, D), D ** -0.5, 0.21875),
        "out_weight": gaussian(key_list[2], (LAYERS, D, D), D ** -0.5, 0.21875),
        "norm_gain": jnp.clip(1.0 + 0.18 * jax.random.normal(key_list[3], (LAYERS, D), jnp.float32), 0.099609375, 1.8984375).astype(jnp.bfloat16),
    }


epsilon = 1e-06

def reference(tokens, qkv_weight, out_weight, norm_gain):
    stream = tokens
    score_scale = 1.0 / (HEAD_DIM * SEQS) ** 0.5
    block_rows = RESIDUES // BLOCKS
    for layer_index in range(LAYERS):
        flattened = stream.reshape(SEQS * RESIDUES, D)
        matrix = qkv_weight[layer_index].reshape(D, 3 * D)
        projected = jnp.dot(flattened, matrix, preferred_element_type=jnp.float32).astype(jnp.bfloat16)
        projected = projected.reshape(SEQS, RESIDUES, 3, HEADS, HEAD_DIM)
        key_vecs = projected[:, :, 1].astype(jnp.float32)
        values = projected[:, :, 2].astype(jnp.float32)
        pieces_out = []
        for block_index in range(BLOCKS):
            queries = projected[:, block_index * block_rows:(block_index + 1) * block_rows, 0].astype(jnp.float32)
            scores = jnp.einsum('sihc,sjhc->hij', queries, key_vecs) * score_scale
            weights = jax.nn.softmax(scores, axis=-1).astype(jnp.bfloat16)
            attended = jnp.einsum('hij,sjhc->sihc', weights.astype(jnp.float32), values)
            pieces_out.append(attended.astype(jnp.bfloat16))
        attended = jnp.concatenate(pieces_out, axis=1).reshape(SEQS * RESIDUES, D)
        update = jnp.dot(attended, out_weight[layer_index], preferred_element_type=jnp.float32)
        summed = flattened.astype(jnp.float32) + update
        mean_sq = lax.optimization_barrier(jnp.mean(summed * summed, axis=-1, keepdims=True))
        normed = summed * lax.rsqrt(mean_sq + epsilon) * norm_gain[layer_index].astype(jnp.float32)
        stream = normed.astype(jnp.bfloat16).reshape(SEQS, RESIDUES, D)
    return stream
```

```python
import functools

import jax
import jax.numpy as jnp
from jax import lax
from jax.experimental import pallas as pl
from jax.experimental.pallas import tpu as pltpu
from jax.sharding import Mesh
from jax.sharding import PartitionSpec as P

D = 768
HEADS = 12
HEAD_DIM = 64
LAYERS = 2
EPSILON = 1e-06
MESH = pl.DeviceIdType.MESH
AXES = ("y", "xh", "z", "xl", "core")
NX, NY, NZ = 4, 4, 8
RES = 512
CORE_HEADS = HEADS // 2
CORE_COLS = CORE_HEADS * HEAD_DIM
QUARTER = D // 4
f32, bf16 = jnp.float32, jnp.bfloat16

RIGHT, LEFT = 0, 1
LONG, SHORT = 0, 1


def wrap(value, n):
    return lax.rem(value + 2 * n, n)


def remote(src, dst, send_sem, recv_sem, device):
    return pltpu.make_async_remote_copy(
        src_ref=src, dst_ref=dst, send_sem=send_sem, recv_sem=recv_sem, device_id=device, device_id_type=MESH
    )


class Ring:
    def __init__(self, n, pos, right, left, send_sems, recv_sems):
        self.n, self.pos, self.devices = n, pos, (right, left)
        self.send_sems, self.recv_sems = send_sems, recv_sems

    def hops(self, kind):
        return self.n // 2 - kind

    def half(self, direction, kind):
        return direction ^ kind

    def index(self, direction, kind, hop):
        return direction * (self.n - 1) + kind * (self.n // 2) + hop - 1

    def owner(self, direction, distance):
        return wrap(self.pos + (distance if direction == RIGHT else -distance), self.n)

    def copy(self, src, dst, direction, i):
        return remote(src, dst, self.send_sems.at[i], self.recv_sems.at[i], self.devices[direction])

    def each(self):
        for kind in (LONG, SHORT):
            for direction in (RIGHT, LEFT):
                yield direction, kind

    def scatter_start(self, view, slot):
        for direction, kind in self.each():
            i = self.index(direction, kind, 1)
            self.copy(
                view(self.owner(direction, self.hops(kind)), self.half(direction, kind)), slot(i), direction, i
            ).start()

    def scatter_event(self, view, slot, kind, hop):
        for direction in (RIGHT, LEFT):
            i = self.index(direction, kind, hop)
            self.copy(slot(i), slot(i), direction, i).wait_recv()
            if hop < self.hops(kind):
                own = view(self.owner(direction, self.hops(kind) - hop), self.half(direction, kind))
                slot(i)[...] = slot(i)[...] + own[...]
                self.copy(slot(i), slot(i + 1), direction, i + 1).start()

    def scatter_result(self, view, slot, half):
        total = view(self.pos, half)[...]
        for direction, kind in self.each():
            if self.half(direction, kind) == half:
                total = total + slot(self.index(direction, kind, self.hops(kind)))[...]
        return total

    def scatter_sent(self, slot):
        for direction, kind in self.each():
            for hop in range(1, self.hops(kind) + 1):
                i = self.index(direction, kind, hop)
                self.copy(slot(i), slot(i), direction, i).wait_send()

    def gather_start(self, view):
        for direction, kind in self.each():
            i = self.index(direction, kind, 1)
            block = view(self.pos, self.half(direction, kind))
            self.copy(block, block, direction, i).start()

    def gather_event(self, view, kind, hop):
        for direction in (RIGHT, LEFT):
            i = self.index(direction, kind, hop)
            block = view(self.owner(direction, -hop), self.half(direction, kind))
            self.copy(block, block, direction, i).wait_recv()
            if hop < self.hops(kind):
                self.copy(block, block, direction, i + 1).start()

    def gather_sent(self, view):
        for direction, kind in self.each():
            block = view(self.pos, self.half(direction, kind))
            for hop in range(1, self.hops(kind) + 1):
                i = self.index(direction, kind, hop)
                self.copy(block, block, direction, i).wait_send()

    def events(self):
        for hop in range(1, self.n // 2 + 1):
            for kind in (LONG, SHORT):
                if hop <= self.hops(kind):
                    yield kind, hop


class Direct:
    def __init__(self, peers, pos, send_sems, recv_sems):
        self.peers, self.pos = peers, pos
        self.send_sems, self.recv_sems = send_sems, recv_sems

    def copy(self, src, dst, k):
        return remote(src, dst, self.send_sems.at[k], self.recv_sems.at[k], self.peers[k][0])

    def scatter_start(self, blocks, slots):
        for k, (_, index) in enumerate(self.peers):
            self.copy(blocks.at[index], slots.at[k], k).start()

    def scatter_result(self, blocks, slots):
        for k in range(len(self.peers)):
            self.copy(slots.at[k], slots.at[k], k).wait_recv()
        total = blocks[self.pos]
        for k in range(len(self.peers)):
            total = total + slots[k]
        return total

    def gather_start(self, blocks):
        for k in range(len(self.peers)):
            self.copy(blocks.at[self.pos], blocks.at[self.pos], k).start()

    def arrived(self, blocks):
        for k in range(len(self.peers)):
            self.copy(blocks.at[self.pos], blocks.at[self.pos], k).wait_recv()

    def sent(self, blocks):
        for k in range(len(self.peers)):
            self.copy(blocks.at[self.pos], blocks.at[self.pos], k).wait_send()


def softmax(scores, scale):
    shifted = (scores - jnp.max(scores, axis=-1, keepdims=True)) * scale
    grown = jnp.exp(shifted)
    return (grown / jnp.sum(grown, axis=-1, keepdims=True)).astype(bf16)


def whole(
    scale, tok, wqkv, wo, gain, out,
    x, wq_in, wo_in, wq_t, wo_t, gain_t, qkv, att,
    s_a, s_b, s_c, r_a, r_b, r_c, acc_a, acc_b, acc_c, r_b2, r_c2, acc_b2, acc_c2, d_a, d_b, d_c,
    w_a, w_b, w_c, g_a, g_b, g_c,
    ss_a, rs_a, ss_b, rs_b, ss_c, rs_c, ss_b2, rs_b2, ss_c2, rs_c2, ss_da, rs_da, ss_db, rs_db, ss_dc, rs_dc,
    sg_a, rg_a, sg_b, rg_b, sg_c, rg_c, sg_b2, rg_b2, sg_c2, rg_c2, sg_da, rg_da, sg_db, rg_db, sg_dc, rg_dc,
    w_sems, x_local, x_send, x_recv, f_send, f_recv, t_send, t_recv, o_local, o_send, o_recv,
):
    y, xh, z = lax.axis_index("y"), lax.axis_index("xh"), lax.axis_index("z")
    xl, core = lax.axis_index("xl"), lax.axis_index("core")
    xpos = xh * 2 + xl

    def at_x(p):
        return {"xh": lax.div(p, 2), "xl": lax.rem(p, 2)}

    x_right, x_left = at_x(wrap(xpos + 1, NX)), at_x(wrap(xpos - 1, NX))
    y_right, y_left = {"y": wrap(y + 1, NY)}, {"y": wrap(y - 1, NY)}
    z_right, z_left = {"z": wrap(z + 1, NZ)}, {"z": wrap(z - 1, NZ)}
    plane = []
    for dx in range(NX):
        for dy in range(NY):
            if dx or dy:
                px, py = wrap(xpos + dx, NX), wrap(y + dy, NY)
                plane.append(({**at_x(px), "y": py}, px * NY + py))
    along_z = [({"z": wrap(z + dz, NZ)}, wrap(z + dz, NZ)) for dz in range(1, NZ)]
    other_core = {"core": 1 - core}
    partner = {"xl": 1 - xl}

    loads = []
    for layer in range(LAYERS):
        for t in range(3):
            loads.append(
                pltpu.make_async_copy(
                    wqkv.at[layer, t, :, pl.ds(pl.multiple_of(core * CORE_COLS, 128), CORE_COLS)],
                    wq_in.at[layer, t],
                    w_sems.at[layer * 4 + t],
                )
            )
        loads.append(pltpu.make_async_copy(wo.at[layer], wo_in.at[layer], w_sems.at[layer * 4 + 3]))
    own_quarter, far_quarter = 2 * xl + core, 2 * (1 - xl) + core
    near_pair, far_pair = 2 * xl, 2 * (1 - xl)

    def quarter(q, offset, size):
        return pl.ds(pl.multiple_of(q * QUARTER + offset, 32), size)

    own_tokens = pltpu.make_async_copy(tok.at[pl.ds(near_pair, 2)], x.at[:, quarter(own_quarter, 0, QUARTER)], x_local)
    own_tokens.start()
    for load in loads:
        load.start()

    barrier = pltpu.get_barrier_semaphore()
    partners = [device for device, _ in plane + along_z] + [other_core]
    for device in partners:
        pl.semaphore_signal(barrier, inc=1, device_id=device, device_id_type=MESH)
    pl.semaphore_wait(barrier, len(partners))

    half_quarter = QUARTER // 2
    pieces = [(s, f) for s in range(2) for f in range(2)]

    def piece(q, s, f):
        return x.at[s, quarter(q, f * half_quarter, half_quarter)]

    for k, (s, f) in enumerate(pieces):
        remote(
            tok.at[far_pair + s, pl.ds(f * half_quarter, half_quarter)], piece(own_quarter, s, f),
            x_send.at[k], x_recv.at[k], partner,
        ).start()
    remote(
        tok.at[pl.ds(near_pair, 2)], x.at[:, quarter(own_quarter, 0, QUARTER)], f_send.at[4], f_recv.at[4], other_core
    ).start()

    for load in loads:
        load.wait()

    def turn(layer, carry):
        for t in range(3):
            wq_t[layer, t] = wq_in[layer, t].T
        for m in range(3):
            wo_t[layer, m * 256 : (m + 1) * 256] = wo_in[layer, :, m * 256 : (m + 1) * 256].T
        return carry

    lax.fori_loop(0, LAYERS, turn, 0)
    for layer in range(LAYERS):
        row = gain[layer : layer + 1, :].astype(f32)
        gain_t[layer] = jnp.broadcast_to(row, (128, D)).T

    for k, (s, f) in enumerate(pieces):
        arrived = piece(far_quarter, s, f)
        remote(arrived, arrived, x_send.at[k], x_recv.at[k], partner).wait_recv()
        remote(arrived, arrived, f_send.at[k], f_recv.at[k], other_core).start()
    own_tokens.wait()
    near = x.at[:, quarter(2 * xl + 1 - core, 0, QUARTER)]
    remote(near, near, f_send.at[4], f_recv.at[4], other_core).wait_recv()
    for k, (s, f) in enumerate(pieces):
        arrived = piece(2 * (1 - xl) + 1 - core, s, f)
        remote(arrived, arrived, f_send.at[k], f_recv.at[k], other_core).wait_recv()
    for k, (s, f) in enumerate(pieces):
        block = piece(far_quarter, s, f)
        remote(block, block, x_send.at[k], x_recv.at[k], partner).wait_send()
        remote(block, block, f_send.at[k], f_recv.at[k], other_core).wait_send()
    near = x.at[:, quarter(own_quarter, 0, QUARTER)]
    remote(near, near, f_send.at[4], f_recv.at[4], other_core).wait_send()

    ring_a = Ring(NZ, z, z_right, z_left, ss_a, rs_a)
    ring_b = Ring(NY, y, y_right, y_left, ss_b, rs_b)
    ring_c = Ring(NX, xpos, x_right, x_left, ss_c, rs_c)
    ring_b2 = Ring(NX, xpos, x_right, x_left, ss_b2, rs_b2)
    ring_c2 = Ring(NY, y, y_right, y_left, ss_c2, rs_c2)
    plane_pos = xpos * NY + y
    direct_a = Direct(plane, plane_pos, ss_da, rs_da)
    direct_b = Direct(along_z, z, ss_db, rs_db)
    direct_c = Direct(along_z, z, ss_dc, rs_dc)
    back_a = Ring(NZ, z, z_right, z_left, sg_a, rg_a)
    back_b = Ring(NY, y, y_right, y_left, sg_b, rg_b)
    back_c = Ring(NX, xpos, x_right, x_left, sg_c, rg_c)
    back_b2 = Ring(NX, xpos, x_right, x_left, sg_b2, rg_b2)
    back_c2 = Ring(NY, y, y_right, y_left, sg_c2, rg_c2)
    spread_a = Direct(plane, plane_pos, sg_da, rg_da)
    spread_b = Direct(along_z, z, sg_db, rg_db)
    spread_c = Direct(along_z, z, sg_dc, rg_dc)

    def pairs(ref):
        return lambda owner, half: ref.at[2 * owner + half]

    def fours(ref):
        return lambda owner, half: ref.at[owner, pl.ds(4 * half, 4)]

    def slots(ref):
        return lambda i: ref.at[i]

    def layer_step(layer, carry):
        def project(t, carry):
            for s in range(2):
                columns = jnp.dot(wq_t[layer, t], x[s], preferred_element_type=f32)
                qkv[t, :, s * HEAD_DIM : (s + 1) * HEAD_DIM, :] = columns.astype(bf16).reshape(
                    CORE_HEADS, HEAD_DIM, RES
                )
            return carry

        lax.fori_loop(0, 3, project, 0)

        def score(first, store):
            def body(h, carry):
                store(
                    h,
                    lax.dot_general(
                        qkv[0, first + h].T, qkv[1, first + h], (((1,), (0,)), ((), ())), preferred_element_type=f32
                    ),
                )
                return carry

            lax.fori_loop(0, 2, body, 0)

        def store_a(h, value):
            s_a[pl.ds(h * 8, 8)] = value.reshape(8, 64, RES)

        def store_b(h, value):
            s_b[pl.ds(h * 2, 2)] = value.reshape(2, 8, 32, RES)

        def store_c(h, value):
            s_c[pl.ds(h * 2, 2)] = value.reshape(2, 8, 32, RES)

        score(0, store_a)
        ring_a.scatter_start(pairs(s_a), slots(r_a))
        score(2, store_b)
        ring_b.scatter_start(fours(s_b), slots(r_b))
        score(4, store_c)
        ring_c.scatter_start(fours(s_c), slots(r_c))

        def step_a(kind, hop):
            ring_a.scatter_event(pairs(s_a), slots(r_a), kind, hop)

        def step_bc(kind, hop):
            ring_b.scatter_event(fours(s_b), slots(r_b), kind, hop)
            ring_c.scatter_event(fours(s_c), slots(r_c), kind, hop)

        def step_bc2(kind, hop):
            ring_b2.scatter_event(pairs(acc_b), slots(r_b2), kind, hop)
            ring_c2.scatter_event(pairs(acc_c), slots(r_c2), kind, hop)

        step_a(LONG, 1)
        step_bc(LONG, 1)
        step_a(SHORT, 1)
        step_a(LONG, 2)
        step_bc(SHORT, 1)
        step_a(SHORT, 2)
        step_a(LONG, 3)
        step_bc(LONG, 2)
        for half in range(2):
            acc_b[4 * half : 4 * half + 4] = ring_b.scatter_result(fours(s_b), slots(r_b), half)
            acc_c[4 * half : 4 * half + 4] = ring_c.scatter_result(fours(s_c), slots(r_c), half)
        ring_b2.scatter_start(pairs(acc_b), slots(r_b2))
        ring_c2.scatter_start(pairs(acc_c), slots(r_c2))
        step_a(SHORT, 3)
        step_bc2(LONG, 1)
        step_a(LONG, 4)
        for half in range(2):
            acc_a[8 * half : 8 * half + 8] = ring_a.scatter_result(pairs(s_a), slots(r_a), half).reshape(8, 8, RES)
        direct_a.scatter_start(acc_a, d_a)
        step_bc2(SHORT, 1)
        step_bc2(LONG, 2)
        for half in range(2):
            acc_b2[4 * half : 4 * half + 4] = ring_b2.scatter_result(pairs(acc_b), slots(r_b2), half).reshape(4, 8, RES)
            acc_c2[4 * half : 4 * half + 4] = ring_c2.scatter_result(pairs(acc_c), slots(r_c2), half).reshape(4, 8, RES)
        direct_b.scatter_start(acc_b2, d_b)
        direct_c.scatter_start(acc_c2, d_c)

        g_a[plane_pos] = softmax(direct_a.scatter_result(acc_a, d_a), scale)
        spread_a.gather_start(g_a)
        g_b[z] = softmax(direct_b.scatter_result(acc_b2, d_b), scale)
        spread_b.gather_start(g_b)
        g_c[z] = softmax(direct_c.scatter_result(acc_c2, d_c), scale)
        ring_a.scatter_sent(slots(r_a))
        ring_b.scatter_sent(slots(r_b))
        ring_c.scatter_sent(slots(r_c))
        ring_b2.scatter_sent(slots(r_b2))
        ring_c2.scatter_sent(slots(r_c2))
        spread_c.gather_start(g_c)

        def joined(ref, first, blocks):
            return ref[first : first + blocks].astype(f32).reshape(blocks * 8, RES).astype(bf16)

        spread_a.arrived(g_a)
        for half in range(2):
            w_a[2 * z + half] = joined(g_a, 8 * half, 8)
        back_a.gather_start(pairs(w_a))
        spread_b.arrived(g_b)
        spread_c.arrived(g_c)
        for half in range(2):
            w_b[y, 2 * xpos + half] = joined(g_b, 4 * half, 4)
            w_c[xpos, 2 * y + half] = joined(g_c, 4 * half, 4)
        view_b2 = lambda owner, half: w_b.at[y, 2 * owner + half]
        view_c2 = lambda owner, half: w_c.at[xpos, 2 * owner + half]
        back_b2.gather_start(view_b2)
        back_c2.gather_start(view_c2)

        def back_bc2(kind, hop):
            back_b2.gather_event(view_b2, kind, hop)
            back_c2.gather_event(view_c2, kind, hop)

        def back_bc(kind, hop):
            back_b.gather_event(fours(w_b), kind, hop)
            back_c.gather_event(fours(w_c), kind, hop)

        back_a.gather_event(pairs(w_a), LONG, 1)
        back_bc2(LONG, 1)
        back_bc2(SHORT, 1)
        back_a.gather_event(pairs(w_a), SHORT, 1)
        back_bc2(LONG, 2)
        back_b.gather_start(fours(w_b))
        back_c.gather_start(fours(w_c))
        back_a.gather_event(pairs(w_a), LONG, 2)
        back_a.gather_event(pairs(w_a), SHORT, 2)
        back_bc(LONG, 1)
        back_a.gather_event(pairs(w_a), LONG, 3)
        back_a.gather_event(pairs(w_a), SHORT, 3)
        back_bc(SHORT, 1)
        back_a.gather_event(pairs(w_a), LONG, 4)

        def attend(first, load):
            def body(h, carry):
                heads = lax.dot_general(
                    qkv[2, first + h], load(h), (((1,), (1,)), ((), ())), preferred_element_type=f32
                ).astype(bf16)
                for s in range(2):
                    at = pl.ds(pl.multiple_of((first + h) * HEAD_DIM, HEAD_DIM), HEAD_DIM)
                    att[layer, s, core, at, :] = heads[s * HEAD_DIM : (s + 1) * HEAD_DIM]
                return carry

            lax.fori_loop(0, 2, body, 0)

        def trade(colour, owner):
            return remote(
                att.at[layer, :, owner, pl.ds(128 * colour, 128)], att.at[layer, :, owner, pl.ds(128 * colour, 128)],
                t_send.at[colour], t_recv.at[layer, colour], other_core,
            )

        attend(0, lambda h: w_a[pl.ds(h * 8, 8)].reshape(RES, RES))
        trade(0, core).start()
        back_bc(LONG, 2)
        attend(2, lambda h: w_b[pl.ds(h * 2, 2)].reshape(RES, RES))
        trade(1, core).start()
        attend(4, lambda h: w_c[pl.ds(h * 2, 2)].reshape(RES, RES))
        trade(2, core).start()

        direct_a.sent(acc_a)
        direct_b.sent(acc_b2)
        direct_c.sent(acc_c2)
        spread_a.sent(g_a)
        spread_b.sent(g_b)
        spread_c.sent(g_c)
        back_a.gather_sent(pairs(w_a))
        back_b.gather_sent(fours(w_b))
        back_c.gather_sent(fours(w_c))
        back_b2.gather_sent(view_b2)
        back_c2.gather_sent(view_c2)

        for colour in range(3):
            trade(colour, 1 - core).wait_recv()
        for colour in range(3):
            trade(colour, core).wait_send()

        def finish(step, carry):
            s = lax.div(step, 2)
            at = pl.ds(pl.multiple_of(lax.rem(step, 2) * 256, 256), 256)
            heads = att[layer, s, :, :, at].reshape(D, 256)
            update = jnp.dot(wo_t[layer], heads, preferred_element_type=f32)
            summed = x[s, :, at].astype(f32) + update
            mean_sq = jnp.mean(summed * summed, axis=0, keepdims=True)
            gains = gain_t[layer]
            normed = summed * lax.rsqrt(mean_sq + EPSILON) * jnp.concatenate([gains, gains], axis=1)
            x[s, :, at] = normed.astype(bf16)
            return carry

        lax.fori_loop(0, 4, finish, 0)
        return carry

    lax.fori_loop(0, LAYERS, layer_step, 0)

    own_out = pltpu.make_async_copy(x.at[:, quarter(own_quarter, 0, QUARTER)], out.at[pl.ds(near_pair, 2)], o_local)
    far_out = remote(
        x.at[:, quarter(far_quarter, 0, QUARTER)], out.at[pl.ds(near_pair, 2)], o_send.at[0], o_recv.at[0], partner
    )
    far_out.start()
    own_out.start()
    own_out.wait()
    far_out.wait_send()
    landed = out.at[pl.ds(far_pair, 2)]
    remote(landed, landed, o_send.at[0], o_recv.at[0], partner).wait_recv()


def on_device(tokens, qkv_weight, out_weight, norm_gain):
    scale = 1.0 / (HEAD_DIM * 2 * NX * NY * NZ) ** 0.5
    any_space = pl.BlockSpec(memory_space=pl.ANY)
    vmem = pl.BlockSpec(memory_space=pltpu.VMEM)
    dma = pltpu.SemaphoreType.DMA
    ring = lambda n: 2 * (n - 1)
    counts = [ring(NZ), ring(NY), ring(NX), ring(NX), ring(NY), NX * NY - 1, NZ - 1, NZ - 1]
    sems = [dma((count,)) for count in counts for _ in range(2)]
    result = pl.pallas_call(
        functools.partial(whole, scale),
        out_shape=jax.ShapeDtypeStruct((4, QUARTER, RES), bf16),
        in_specs=[any_space, any_space, any_space, vmem],
        out_specs=any_space,
        scratch_shapes=[
            pltpu.VMEM((2, D, RES), bf16),
            pltpu.VMEM((LAYERS, 3, D, CORE_COLS), bf16),
            pltpu.VMEM((LAYERS, D, D), bf16),
            pltpu.VMEM((LAYERS, 3, CORE_COLS, D), bf16),
            pltpu.VMEM((LAYERS, D, D), bf16),
            pltpu.VMEM((LAYERS, D, 128), f32),
            pltpu.VMEM((3, CORE_HEADS, 2 * HEAD_DIM, RES), bf16),
            pltpu.VMEM((LAYERS, 2, 2, CORE_COLS, RES), bf16),
            pltpu.VMEM((16, 64, RES), f32),
            pltpu.VMEM((4, 8, 32, RES), f32),
            pltpu.VMEM((4, 8, 32, RES), f32),
            pltpu.VMEM((14, 64, RES), f32),
            pltpu.VMEM((6, 4, 32, RES), f32),
            pltpu.VMEM((6, 4, 32, RES), f32),
            pltpu.VMEM((16, 8, RES), f32),
            pltpu.VMEM((8, 32, RES), f32),
            pltpu.VMEM((8, 32, RES), f32),
            pltpu.VMEM((6, 32, RES), f32),
            pltpu.VMEM((6, 32, RES), f32),
            pltpu.VMEM((8, 8, RES), f32),
            pltpu.VMEM((8, 8, RES), f32),
            pltpu.VMEM((15, 8, RES), f32),
            pltpu.VMEM((7, 8, RES), f32),
            pltpu.VMEM((7, 8, RES), f32),
            pltpu.VMEM((16, 64, RES), bf16),
            pltpu.VMEM((4, 8, 32, RES), bf16),
            pltpu.VMEM((4, 8, 32, RES), bf16),
            pltpu.VMEM((16, 8, RES), bf16),
            pltpu.VMEM((8, 8, RES), bf16),
            pltpu.VMEM((8, 8, RES), bf16),
            *sems,
            *sems,
            dma((4 * LAYERS,)),
            dma,
            dma((4,)),
            dma((4,)),
            dma((5,)),
            dma((5,)),
            dma((3,)),
            dma((LAYERS, 3)),
            dma,
            dma((1,)),
            dma((1,)),
        ],
        compiler_params=pltpu.CompilerParams(
            collective_id=0, has_side_effects=True, vmem_limit_bytes=60 * 1024 * 1024
        ),
    )(
        tokens.transpose(0, 2, 1),
        qkv_weight.transpose(0, 2, 1, 3),
        out_weight,
        norm_gain,
    )
    return result.transpose(0, 2, 1)


def solution(mesh):
    finer = Mesh(mesh.devices.reshape(NY, NX // 2, NZ, 2, 2), AXES)
    rows, heads = ("y", "xh", "z"), ("xl", "core")
    return jax.shard_map(
        on_device,
        mesh=finer,
        in_specs=(P(rows, None, heads), P(), P(), P()),
        out_specs=P(rows, None, heads),
        check_vma=False,
    )
```

```python
import functools

import jax
import jax.numpy as jnp
from jax import lax
from jax.experimental import pallas as pl
from jax.experimental.pallas import tpu as pltpu
from jax.sharding import Mesh
from jax.sharding import PartitionSpec as P

D = 768
HEADS = 12
HEAD_DIM = 64
LAYERS = 2
EPSILON = 1e-06
MESH = pl.DeviceIdType.MESH
AXES = ("y", "xh", "z", "xl", "core")
NX, NY, NZ = 4, 4, 8
RES = 512
BLOCK = RES // 2
CORE_HEADS = HEADS // 2
CORE_COLS = CORE_HEADS * HEAD_DIM
QUARTER = D // 4
f32, bf16 = jnp.float32, jnp.bfloat16

RIGHT, LEFT = 0, 1
LONG, SHORT = 0, 1


def wrap(value, n):
    return lax.rem(value + 2 * n, n)


def remote(src, dst, send_sem, recv_sem, device):
    return pltpu.make_async_remote_copy(
        src_ref=src, dst_ref=dst, send_sem=send_sem, recv_sem=recv_sem, device_id=device, device_id_type=MESH
    )


class Clock:
    RATE, FIRST_HOP, NEXT_HOP = 54e3, 2.2, 0.63

    def __init__(self):
        self.now, self.free = 0.0, {}

    def spend(self, time):
        self.now += time

    def send(self, link, size, hops=1):
        begin = max(self.now, self.free.get(link, 0.0))
        self.free[link] = begin + size / self.RATE
        return self.free[link] + self.FIRST_HOP + self.NEXT_HOP * (hops - 1)


class Ring:
    def __init__(self, clock, axis, size, n, pos, right, left, send_sems, recv_sems):
        self.clock, self.axis, self.size = clock, axis, size
        self.n, self.pos, self.devices = n, pos, (right, left)
        self.send_sems, self.recv_sems = send_sems, recv_sems
        self.due = {}

    def hops(self, kind):
        return self.n // 2 - kind

    def half(self, direction, kind):
        return direction ^ kind

    def index(self, direction, kind, hop):
        return direction * (self.n - 1) + kind * (self.n // 2) + hop - 1

    def owner(self, direction, distance):
        return wrap(self.pos + (distance if direction == RIGHT else -distance), self.n)

    def copy(self, src, dst, direction, i):
        return remote(src, dst, self.send_sems(i), self.recv_sems(i), self.devices[direction])

    def start(self, src, dst, direction, kind, hop):
        self.copy(src, dst, direction, self.index(direction, kind, hop)).start()
        self.due[kind, hop] = self.clock.send((self.axis, direction), self.size)

    def each(self):
        for kind in (LONG, SHORT):
            for direction in (RIGHT, LEFT):
                yield direction, kind

    def events(self):
        for hop in range(1, self.n // 2 + 1):
            for kind in (LONG, SHORT):
                if hop <= self.hops(kind):
                    yield kind, hop

    def scatter(self, view, slot, after_first=None):
        for direction, kind in self.each():
            own = view(self.owner(direction, self.hops(kind)), self.half(direction, kind))
            self.start(own, slot(self.index(direction, kind, 1)), direction, kind, 1)
        for kind, hop in self.events():
            yield self.due[kind, hop]
            for direction in (RIGHT, LEFT):
                i = self.index(direction, kind, hop)
                self.copy(slot(i), slot(i), direction, i).wait_recv()
                if hop < self.hops(kind):
                    own = view(self.owner(direction, self.hops(kind) - hop), self.half(direction, kind))
                    slot(i)[...] = slot(i)[...] + own[...]
                    self.start(slot(i), slot(i + 1), direction, kind, hop + 1)
            self.clock.spend(self.size / 500e3)
            if after_first is not None and (kind, hop) == (LONG, 1):
                after_first()

    def scatter_result(self, view, slot, half):
        total = view(self.pos, half)[...]
        for direction, kind in self.each():
            if self.half(direction, kind) == half:
                total = total + slot(self.index(direction, kind, self.hops(kind)))[...]
        return total

    def scatter_sent(self, slot):
        for direction, kind in self.each():
            for hop in range(1, self.hops(kind) + 1):
                i = self.index(direction, kind, hop)
                self.copy(slot(i), slot(i), direction, i).wait_send()

    def gather(self, view):
        for direction, kind in self.each():
            block = view(self.pos, self.half(direction, kind))
            self.start(block, block, direction, kind, 1)
        for kind, hop in self.events():
            yield self.due[kind, hop]
            for direction in (RIGHT, LEFT):
                i = self.index(direction, kind, hop)
                block = view(self.owner(direction, -hop), self.half(direction, kind))
                self.copy(block, block, direction, i).wait_recv()
                if hop < self.hops(kind):
                    self.start(block, block, direction, kind, hop + 1)

    def gather_sent(self, view):
        for direction, kind in self.each():
            block = view(self.pos, self.half(direction, kind))
            for hop in range(1, self.hops(kind) + 1):
                i = self.index(direction, kind, hop)
                self.copy(block, block, direction, i).wait_send()


class Direct:
    def __init__(self, clock, size, peers, pos, owns, send_sems, recv_sems):
        self.clock, self.size, self.peers, self.pos, self.owns = clock, size, peers, pos, owns
        self.send_sems, self.recv_sems = send_sems, recv_sems

    def copy(self, src, dst, k):
        return remote(src, dst, self.send_sems(k), self.recv_sems(k), self.peers[k][0])

    def to_owners(self, action):
        same = [k for k, peer in enumerate(self.peers) if peer[2]]
        other = [k for k, peer in enumerate(self.peers) if not peer[2]]

        @pl.when(self.owns)
        def _():
            for k in same:
                action(k)

        @pl.when(jnp.logical_not(self.owns))
        def _():
            for k in other:
                action(k)

    def price(self, count):
        return max(
            self.clock.send(link, self.size * count / len(self.peers), hops) for _, _, _, link, hops in self.peers
        )

    def scatter_start(self, blocks, slots):
        self.to_owners(lambda k: self.copy(blocks.at[self.peers[k][1]], slots(k), k).start())
        return self.price(len(self.peers) // 2)

    def turn(self, blocks, slots, spread, weights, scale):
        every = range(len(self.peers))

        @pl.when(self.owns)
        def _():
            for k in every:
                self.copy(slots(k), slots(k), k).wait_recv()
            total = blocks[self.pos]
            for k in every:
                total = total + slots(k)[...]
            weights[self.pos] = softmax(total, scale)
            for k in every:
                spread.copy(weights.at[self.pos], weights.at[self.pos], k).start()

        self.clock.spend(0.6)
        return spread.price(len(self.peers) // 2)

    def arrived(self, blocks):
        self.to_owners(lambda k: self.copy(blocks.at[self.pos], blocks.at[self.pos], k).wait_recv())

    def scatter_sent(self, blocks):
        self.to_owners(lambda k: self.copy(blocks.at[self.pos], blocks.at[self.pos], k).wait_send())

    def gather_sent(self, blocks):
        @pl.when(self.owns)
        def _():
            for k in range(len(self.peers)):
                self.copy(blocks.at[self.pos], blocks.at[self.pos], k).wait_send()


def softmax(scores, scale):
    shifted = (scores - jnp.max(scores, axis=-1, keepdims=True)) * scale
    grown = jnp.exp(shifted)
    return (grown / jnp.sum(grown, axis=-1, keepdims=True)).astype(bf16)


def whole(
    scale, tok, wqkv, wo, gain, out,
    x, wq_in, wo_in, wq_t, wo_t, gain_t, qkv, att,
    s_a, s_b, s_c, r_a, r_b, r_c, acc_a, acc_b, acc_c, r_b2, r_c2, acc_b2, acc_c2, d_a, d_b, d_c,
    w_a, w_b, w_c, g_a, g_b, g_c, ring_sems, direct_sems,
    w_sems, x_local, x_send, x_recv, f_send, f_recv, t_send, t_recv, o_local, o_send, o_recv,
):
    y, xh, z = lax.axis_index("y"), lax.axis_index("xh"), lax.axis_index("z")
    xl, core = lax.axis_index("xl"), lax.axis_index("core")
    xpos = xh * 2 + xl

    def at_x(p):
        return {"xh": lax.div(p, 2), "xl": lax.rem(p, 2)}

    x_right, x_left = at_x(wrap(xpos + 1, NX)), at_x(wrap(xpos - 1, NX))
    y_right, y_left = {"y": wrap(y + 1, NY)}, {"y": wrap(y - 1, NY)}
    z_right, z_left = {"z": wrap(z + 1, NZ)}, {"z": wrap(z - 1, NZ)}
    plane = []
    for dx in range(NX):
        for dy in range(NY):
            if dx or dy:
                px, py = wrap(xpos + dx, NX), wrap(y + dy, NY)
                link = ("x", int(dx > NX // 2)) if dx else ("y", int(dy > NY // 2))
                far = min(dx, NX - dx) + min(dy, NY - dy)
                index = px * (NY // 2) + lax.div(py, 2)
                plane.append(({**at_x(px), "y": py}, index, (dx + dy) % 2 == 0, link, far))
    along_z = []
    for dz in range(1, NZ):
        pz = wrap(z + dz, NZ)
        along_z.append(({"z": pz}, lax.div(pz, 2), dz % 2 == 0, ("z", int(dz > NZ // 2)), min(dz, NZ - dz)))
    other_core = {"core": 1 - core}
    partner = {"xl": 1 - xl}

    loads = []
    for layer in range(LAYERS):
        for t in range(3):
            loads.append(
                pltpu.make_async_copy(
                    wqkv.at[layer, t, :, pl.ds(pl.multiple_of(core * CORE_COLS, 128), CORE_COLS)],
                    wq_in.at[layer, t],
                    w_sems.at[layer * 4 + t],
                )
            )
        loads.append(pltpu.make_async_copy(wo.at[layer], wo_in.at[layer], w_sems.at[layer * 4 + 3]))
    own_quarter, far_quarter = 2 * xl + core, 2 * (1 - xl) + core
    near_pair, far_pair = 2 * xl, 2 * (1 - xl)

    def quarter(q):
        return pl.ds(pl.multiple_of(q * QUARTER, 64), QUARTER)

    own_tokens = pltpu.make_async_copy(tok.at[pl.ds(near_pair, 2)], x.at[:, quarter(own_quarter)], x_local)
    own_tokens.start()
    for load in loads:
        load.start()

    barrier = pltpu.get_barrier_semaphore()
    partners = [peer[0] for peer in plane + along_z] + [other_core]
    for device in partners:
        pl.semaphore_signal(barrier, inc=1, device_id=device, device_id_type=MESH)
    pl.semaphore_wait(barrier, len(partners))

    def block(b):
        return slice(b * BLOCK, (b + 1) * BLOCK)

    pieces = [(b, s) for b in range(2) for s in range(2)]

    def piece(q, b, s):
        return x.at[s, quarter(q), block(b)]

    for k, (b, s) in enumerate(pieces):
        remote(
            tok.at[far_pair + s, :, block(b)], piece(own_quarter, b, s), x_send.at[k], x_recv.at[k], partner
        ).start()
    remote(
        tok.at[pl.ds(near_pair, 2)], x.at[:, quarter(own_quarter)], f_send.at[4], f_recv.at[4], other_core
    ).start()

    def turn_columns(layer, t):
        loads[layer * 4 + t].wait()
        wq_t[layer, t] = wq_in[layer, t].T

    def turn_out(layer):
        loads[layer * 4 + 3].wait()
        for m in range(3):
            wo_t[layer, m * 256 : (m + 1) * 256] = wo_in[layer, :, m * 256 : (m + 1) * 256].T
        row = gain[layer : layer + 1, :].astype(f32)
        gain_t[layer] = jnp.broadcast_to(row, (128, D)).T

    clock = Clock()

    def project(layer, t, b):
        for s in range(2):
            columns = jnp.dot(wq_t[layer, t], x[s, :, block(b)], preferred_element_type=f32)
            qkv[layer, t, :, s * HEAD_DIM : (s + 1) * HEAD_DIM, block(b)] = columns.astype(bf16).reshape(
                CORE_HEADS, HEAD_DIM, BLOCK
            )
        clock.spend(0.5)

    turn_columns(0, 0)
    turn_columns(0, 1)
    for k, (b, s) in enumerate(pieces):
        arrived = piece(far_quarter, b, s)
        remote(arrived, arrived, x_send.at[k], x_recv.at[k], partner).wait_recv()
        remote(arrived, arrived, f_send.at[k], f_recv.at[k], other_core).start()
        if k == 0:
            turn_columns(0, 2)
            own_tokens.wait()
            near = x.at[:, quarter(2 * xl + 1 - core)]
            remote(near, near, f_send.at[4], f_recv.at[4], other_core).wait_recv()
        if k == 2:
            for j in range(2):
                arrived = piece(2 * (1 - xl) + 1 - core, *pieces[j])
                remote(arrived, arrived, f_send.at[j], f_recv.at[j], other_core).wait_recv()
            project(0, 0, 0)
            project(0, 1, 0)
    for j in range(2, 4):
        arrived = piece(2 * (1 - xl) + 1 - core, *pieces[j])
        remote(arrived, arrived, f_send.at[j], f_recv.at[j], other_core).wait_recv()
    project(0, 0, 1)
    project(0, 1, 1)

    def tokens_sent():
        for k, (b, s) in enumerate(pieces):
            arrived = piece(far_quarter, b, s)
            remote(arrived, arrived, x_send.at[k], x_recv.at[k], partner).wait_send()
            remote(arrived, arrived, f_send.at[k], f_recv.at[k], other_core).wait_send()
        near = x.at[:, quarter(own_quarter)]
        remote(near, near, f_send.at[4], f_recv.at[4], other_core).wait_send()

    plane_pos = xpos * (NY // 2) + lax.div(y, 2)
    z_pos = lax.div(z, 2)
    plane_parity, z_parity = lax.rem(xpos + y, 2), lax.rem(z, 2)

    def taker(table):
        taken = [0]

        def take(count):
            first = taken[0]
            taken[0] += count
            return lambda i: table.at[first + i]

        return take

    row = RES * 4

    def colour_rings(b):
        take_ring, take_direct = taker(ring_sems.at[b]), taker(direct_sems.at[b])

        def ring(axis, rows, width):
            n, pos, right, left = {
                "x": (NX, xpos, x_right, x_left),
                "y": (NY, y, y_right, y_left),
                "z": (NZ, z, z_right, z_left),
            }[axis]
            count = 2 * (n - 1)
            return Ring(clock, axis, rows * row * width, n, pos, right, left, take_ring(count), take_ring(count))

        def direct(peers, width):
            pos, parity = (plane_pos, plane_parity) if peers is plane else (z_pos, z_parity)
            return Direct(
                clock, 8 * row * width, peers, pos, parity == b, take_direct(len(peers)), take_direct(len(peers))
            )

        return [
            dict(
                down=[ring("z", 32, 1)], owners=direct(plane, 1), spread=direct(plane, 0.5), up=[ring("z", 32, 0.5)]
            )
        ] + [
            dict(
                down=[ring(first, 64, 1), ring(second, 16, 1)],
                owners=direct(along_z, 1),
                spread=direct(along_z, 0.5),
                up=[ring(second, 16, 0.5), ring(first, 64, 0.5)],
            )
            for first, second in (("y", "x"), ("x", "y"))
        ]

    groups = [colour_rings(b) for b in range(2)]

    def slots(ref, b):
        return lambda i: ref.at[b, i]

    def pairs(ref, b):
        return lambda owner, half: ref.at[b, 2 * owner + half]

    def fours(ref, b):
        return lambda owner, half: ref.at[b, owner, pl.ds(4 * half, 4)]

    places = [
        dict(s=s_a, r=r_a, r2=None, acc=None, last=acc_a, d=d_a, w=w_a, g=g_a, view=pairs, blocks=(8, 32)),
        dict(s=s_b, r=r_b, r2=r_b2, acc=acc_b, last=acc_b2, d=d_b, w=w_b, g=g_b, view=fours, blocks=(2, 8, 16)),
        dict(s=s_c, r=r_c, r2=r_c2, acc=acc_c, last=acc_c2, d=d_c, w=w_c, g=g_c, view=fours, blocks=(2, 8, 16)),
    ]
    middle = [None, lambda b: lambda owner, half: w_b.at[b, y, 2 * owner + half],
              lambda b: lambda owner, half: w_c.at[b, xpos, 2 * owner + half]]

    def trade(layer, b, colour, owner):
        part = att.at[layer, :, owner, pl.ds(128 * colour, 128), block(b)]
        return remote(part, part, t_send.at[b, colour], t_recv.at[layer, b, colour], other_core)

    def score(layer, b, colour):
        place = places[colour]
        blocks = place["blocks"]

        def body(h, carry):
            head = 2 * colour + h
            scores = jnp.dot(
                qkv[layer, 0, head, :, block(b)].T, qkv[layer, 1, head], preferred_element_type=f32
            )
            place["s"][b, pl.ds(h * blocks[0], blocks[0])] = scores.reshape(*blocks, RES)
            return carry

        lax.fori_loop(0, 2, body, 0)
        clock.spend(0.5)

    def attend(layer, b, colour):
        place = places[colour]
        blocks = place["blocks"]

        def body(h, carry):
            head = 2 * colour + h
            weights = place["w"][b, pl.ds(h * blocks[0], blocks[0])].reshape(BLOCK, RES)
            heads = lax.dot_general(
                qkv[layer, 2, head], weights, (((1,), (1,)), ((), ())), preferred_element_type=f32
            ).astype(bf16)
            at = pl.ds(pl.multiple_of(head * HEAD_DIM, HEAD_DIM), HEAD_DIM)
            for s in range(2):
                att[layer, s, core, at, block(b)] = heads[s * HEAD_DIM : (s + 1) * HEAD_DIM]
            return carry

        lax.fori_loop(0, 2, body, 0)
        clock.spend(0.6)

    def joined(ref, b, first, blocks):
        return ref[b, first : first + blocks].astype(f32).reshape(blocks * 8, RES).astype(bf16)

    def colour_steps(layer, b, colour, after_first, done):
        place, group = places[colour], groups[b][colour]
        view, slot = place["view"](place["s"], b), slots(place["r"], b)
        score(layer, b, colour)
        down = group["down"]
        yield from down[0].scatter(view, slot, after_first)
        last = place["last"].at[b]
        if colour == 0:
            for half in range(2):
                last[4 * half : 4 * half + 4] = down[0].scatter_result(view, slot, half).reshape(4, 8, RES)
        else:
            view2, slot2 = pairs(place["acc"], b), slots(place["r2"], b)
            for half in range(2):
                place["acc"][b, 4 * half : 4 * half + 4] = down[0].scatter_result(view, slot, half)
            yield from down[1].scatter(view2, slot2)
            for half in range(2):
                last[2 * half : 2 * half + 2] = down[1].scatter_result(view2, slot2, half).reshape(2, 8, RES)
            down[1].scatter_sent(slot2)
        down[0].scatter_sent(slot)
        yield group["owners"].scatter_start(last, slots(place["d"], b))
        yield group["owners"].turn(last, slots(place["d"], b), group["spread"], place["g"].at[b], scale)
        group["spread"].arrived(place["g"].at[b])
        w, up = place["w"], group["up"]
        if colour == 0:
            for half in range(2):
                w[b, 2 * z + half] = joined(place["g"], b, 4 * half, 4)
        else:
            first, second = (y, xpos) if colour == 1 else (xpos, y)
            for half in range(2):
                w[b, first, 2 * second + half] = joined(place["g"], b, 2 * half, 2)
            yield from up[0].gather(middle[colour](b))
        yield from up[-1].gather(place["view"](w, b))
        attend(layer, b, colour)
        trade(layer, b, colour, core).start()
        done()

    def all_sent(b):
        for colour in range(3):
            place, group = places[colour], groups[b][colour]
            group["owners"].scatter_sent(place["last"].at[b])
            group["spread"].gather_sent(place["g"].at[b])
            group["up"][-1].gather_sent(place["view"](place["w"], b))
            if colour:
                group["up"][0].gather_sent(middle[colour](b))

    def finish(layer, b):
        def body(s, carry):
            heads = att[layer, s, :, :, block(b)].reshape(D, BLOCK)
            update = jnp.dot(wo_t[layer], heads, preferred_element_type=f32)
            summed = x[s, :, block(b)].astype(f32) + update
            mean_sq = jnp.mean(summed * summed, axis=0, keepdims=True)
            gains = gain_t[layer]
            normed = summed * lax.rsqrt(mean_sq + EPSILON) * jnp.concatenate([gains, gains], axis=1)
            x[s, :, block(b)] = normed.astype(bf16)
            return carry

        lax.fori_loop(0, 2, body, 0)
        clock.spend(1.5)

    def far_out(b):
        return remote(
            x.at[:, quarter(far_quarter), block(b)], out.at[pl.ds(near_pair, 2), :, block(b)],
            o_send.at[b], o_recv.at[b], partner,
        )

    def own_out(b):
        return pltpu.make_async_copy(
            x.at[:, quarter(own_quarter), block(b)], out.at[pl.ds(near_pair, 2), :, block(b)], o_local.at[b]
        )

    def finish_steps(layer, b):
        yield clock.now + 1.6
        for colour in range(3):
            trade(layer, b, colour, 1 - core).wait_recv()
        finish(layer, b)
        if layer + 1 < LAYERS:
            project(layer + 1, 0, b)
            project(layer + 1, 1, b)
        else:
            far_out(b).start()
            own_out(b).start()

    for layer in range(LAYERS):
        running, order = [], [0]

        def add(steps, running=running, order=order):
            due = next(steps, None)
            if due is not None:
                order[0] += 1
                running.append((due, order[0], steps))

        def launch(b, colour, layer=layer, add=add):
            left[b][colour] = 1

            def after_first():
                if b == 0:
                    launch(1, colour)

            def done():
                left[b][colour] = 0
                if sum(left[b].values()) == 0 and len(left[b]) == 3:
                    add(finish_steps(layer, b))

            add(colour_steps(layer, b, colour, after_first, done))

        left = [{}, {}]
        for colour in range(3):
            launch(0, colour)
        for b in range(2):
            project(layer, 2, b)
        fillers = []
        if layer == 0:
            tokens_sent()
            fillers = [functools.partial(turn_out, 0)]
            fillers += [functools.partial(turn_columns, 1, t) for t in range(3)]
            fillers += [functools.partial(turn_out, 1)]
        while running:
            running.sort(key=lambda entry: entry[:2])
            if fillers and running[0][0] > clock.now + 0.7:
                fillers.pop(0)()
                clock.spend(1.0)
                continue
            due, _, steps = running.pop(0)
            clock.now = max(clock.now, due)
            add(steps)
        for filler in fillers:
            filler()
        for b in range(2):
            all_sent(b)
            for colour in range(3):
                trade(layer, b, colour, core).wait_send()

    for b in range(2):
        own_out(b).wait()
        far_out(b).wait_send()
        landed = out.at[pl.ds(far_pair, 2), :, block(b)]
        remote(landed, landed, o_send.at[b], o_recv.at[b], partner).wait_recv()


def on_device(tokens, qkv_weight, out_weight, norm_gain):
    scale = 1.0 / (HEAD_DIM * 2 * NX * NY * NZ) ** 0.5
    any_space = pl.BlockSpec(memory_space=pl.ANY)
    vmem = pl.BlockSpec(memory_space=pltpu.VMEM)
    dma = pltpu.SemaphoreType.DMA
    around = lambda n: 2 * (n - 1)
    ring_count = 4 * (around(NZ) + 2 * around(NX) + 2 * around(NY))
    direct_count = 4 * (NX * NY - 1 + 2 * (NZ - 1))
    result = pl.pallas_call(
        functools.partial(whole, scale),
        out_shape=jax.ShapeDtypeStruct((4, QUARTER, RES), bf16),
        in_specs=[any_space, any_space, any_space, vmem],
        out_specs=vmem,
        scratch_shapes=[
            pltpu.VMEM((2, D, RES), bf16),
            pltpu.VMEM((LAYERS, 3, D, CORE_COLS), bf16),
            pltpu.VMEM((LAYERS, D, D), bf16),
            pltpu.VMEM((LAYERS, 3, CORE_COLS, D), bf16),
            pltpu.VMEM((LAYERS, D, D), bf16),
            pltpu.VMEM((LAYERS, D, 128), f32),
            pltpu.VMEM((LAYERS, 3, CORE_HEADS, 2 * HEAD_DIM, RES), bf16),
            pltpu.VMEM((LAYERS, 2, 2, CORE_COLS, RES), bf16),
            pltpu.VMEM((2, 16, 32, RES), f32),
            pltpu.VMEM((2, 4, 8, 16, RES), f32),
            pltpu.VMEM((2, 4, 8, 16, RES), f32),
            pltpu.VMEM((2, 14, 32, RES), f32),
            pltpu.VMEM((2, 6, 4, 16, RES), f32),
            pltpu.VMEM((2, 6, 4, 16, RES), f32),
            pltpu.VMEM((2, 8, 8, RES), f32),
            pltpu.VMEM((2, 8, 16, RES), f32),
            pltpu.VMEM((2, 8, 16, RES), f32),
            pltpu.VMEM((2, 6, 16, RES), f32),
            pltpu.VMEM((2, 6, 16, RES), f32),
            pltpu.VMEM((2, 4, 8, RES), f32),
            pltpu.VMEM((2, 4, 8, RES), f32),
            pltpu.VMEM((2, 15, 8, RES), f32),
            pltpu.VMEM((2, 7, 8, RES), f32),
            pltpu.VMEM((2, 7, 8, RES), f32),
            pltpu.VMEM((2, 16, 32, RES), bf16),
            pltpu.VMEM((2, 4, 8, 16, RES), bf16),
            pltpu.VMEM((2, 4, 8, 16, RES), bf16),
            pltpu.VMEM((2, 8, 8, RES), bf16),
            pltpu.VMEM((2, 4, 8, RES), bf16),
            pltpu.VMEM((2, 4, 8, RES), bf16),
            dma((2, ring_count)),
            dma((2, direct_count)),
            dma((4 * LAYERS,)),
            dma,
            dma((4,)),
            dma((4,)),
            dma((5,)),
            dma((5,)),
            dma((2, 3)),
            dma((LAYERS, 2, 3)),
            dma((2,)),
            dma((2,)),
            dma((2,)),
        ],
        compiler_params=pltpu.CompilerParams(
            collective_id=0, has_side_effects=True, vmem_limit_bytes=60 * 1024 * 1024
        ),
    )(
        tokens.transpose(0, 2, 1),
        qkv_weight.transpose(0, 2, 1, 3),
        out_weight,
        norm_gain,
    )
    return result.transpose(0, 2, 1)


def solution(mesh):
    finer = Mesh(mesh.devices.reshape(NY, NX // 2, NZ, 2, 2), AXES)
    rows, heads = ("y", "xh", "z"), ("xl", "core")
    return jax.shard_map(
        on_device,
        mesh=finer,
        in_specs=(P(rows, None, heads), P(), P(), P()),
        out_specs=P(rows, None, heads),
        check_vma=False,
    )
```

```python
import functools

import jax
import jax.numpy as jnp
from jax import lax
from jax.experimental import pallas as pl
from jax.experimental.pallas import tpu as pltpu
from jax.sharding import Mesh
from jax.sharding import PartitionSpec as P

D = 768
HEADS = 12
HEAD_DIM = 64
LAYERS = 2
EPSILON = 1e-06
MESH = pl.DeviceIdType.MESH
AXES = ("y", "xh", "z", "xl", "core")
NX, NY, NZ = 4, 4, 8
RES = 512
BLOCK = RES // 2
CORE_HEADS = HEADS // 2
CORE_COLS = CORE_HEADS * HEAD_DIM
QUARTER = D // 4
f32, bf16 = jnp.float32, jnp.bfloat16

RIGHT, LEFT = 0, 1
LONG, SHORT = 0, 1


def wrap(value, n):
    return lax.rem(value + 2 * n, n)


def remote(src, dst, send_sem, recv_sem, device):
    return pltpu.make_async_remote_copy(
        src_ref=src, dst_ref=dst, send_sem=send_sem, recv_sem=recv_sem, device_id=device, device_id_type=MESH
    )


STEPS = 195.0
LOWEST = 100.0


def encode(value):
    rows, columns = value.shape
    size = jnp.abs(value)
    top = functools.reduce(
        jnp.maximum,
        [size[r : r + 8, c : c + 128] for r in range(0, rows, 8) for c in range(0, columns, 128)],
    )
    top = jnp.maximum(top, 1e-30)
    per_unit = jnp.concatenate([STEPS / top] * (columns // 128), axis=1)
    per_unit = jnp.concatenate([per_unit] * (rows // 8), axis=0)
    level = size * per_unit
    binade = jnp.floor(level)
    code = (1.0 + (level - binade)) * jnp.exp2(binade - LOWEST)
    return jnp.where(value < 0, -code, code).astype(bf16), top / STEPS


def decode(code, unit):
    rows, columns = code.shape
    code = code.astype(f32)
    size = jnp.abs(code)
    binade = jnp.floor(jnp.log2(size))
    level = binade + size * jnp.exp2(-binade) + (LOWEST - 1.0)
    unit = jnp.concatenate([unit] * (columns // 128), axis=1)
    unit = jnp.concatenate([unit] * (rows // 8), axis=0)
    return jnp.where(code < 0, -level, level) * unit


class Clock:
    RATE, FIRST_HOP, NEXT_HOP = 46e3, 2.6, 0.65

    def __init__(self):
        self.now, self.free = 0.0, {}

    def spend(self, time):
        self.now += time

    def send(self, link, size, hops=1):
        begin = max(self.now, self.free.get(link, 0.0))
        self.free[link] = begin + size / self.RATE
        return self.free[link] + self.FIRST_HOP + self.NEXT_HOP * (hops - 1)


class Ring:
    def __init__(self, clock, axis, size, n, pos, right, left, send_sems, recv_sems):
        self.clock, self.axis, self.size = clock, axis, size
        self.n, self.pos, self.devices = n, pos, (right, left)
        self.send_sems, self.recv_sems = send_sems, recv_sems
        self.due = {}

    def hops(self, kind):
        return self.n // 2 - kind

    def half(self, direction, kind):
        return direction ^ kind

    def index(self, direction, kind, hop):
        return direction * (self.n - 1) + kind * (self.n // 2) + hop - 1

    def owner(self, direction, distance):
        return wrap(self.pos + (distance if direction == RIGHT else -distance), self.n)

    def copy(self, src, dst, direction, i):
        return remote(src, dst, self.send_sems(i), self.recv_sems(i), self.devices[direction])

    def start(self, src, dst, direction, kind, hop):
        self.copy(src, dst, direction, self.index(direction, kind, hop)).start()
        self.due[kind, hop] = self.clock.send((self.axis, direction), self.size)

    def each(self):
        for kind in (LONG, SHORT):
            for direction in (RIGHT, LEFT):
                yield direction, kind

    def events(self):
        for hop in range(1, self.n // 2 + 1):
            for kind in (LONG, SHORT):
                if hop <= self.hops(kind):
                    yield kind, hop

    def scatter(self, view, slot, after_first=None):
        for direction, kind in self.each():
            own = view(self.owner(direction, self.hops(kind)), self.half(direction, kind))
            self.start(own, slot(self.index(direction, kind, 1)), direction, kind, 1)
        for kind, hop in self.events():
            yield self.due[kind, hop]
            for direction in (RIGHT, LEFT):
                i = self.index(direction, kind, hop)
                self.copy(slot(i), slot(i), direction, i).wait_recv()
                if hop < self.hops(kind):
                    own = view(self.owner(direction, self.hops(kind) - hop), self.half(direction, kind))
                    slot(i)[...] = slot(i)[...] + own[...]
                    self.start(slot(i), slot(i + 1), direction, kind, hop + 1)
            self.clock.spend(self.size / 500e3)
            if after_first is not None and (kind, hop) == (LONG, 1):
                after_first()

    def scatter_result(self, view, slot, half):
        total = view(self.pos, half)[...]
        for direction, kind in self.each():
            if self.half(direction, kind) == half:
                total = total + slot(self.index(direction, kind, self.hops(kind)))[...]
        return total

    def scatter_sent(self, slot):
        for direction, kind in self.each():
            for hop in range(1, self.hops(kind) + 1):
                i = self.index(direction, kind, hop)
                self.copy(slot(i), slot(i), direction, i).wait_send()

    def gather(self, view):
        for direction, kind in self.each():
            block = view(self.pos, self.half(direction, kind))
            self.start(block, block, direction, kind, 1)
        for kind, hop in self.events():
            yield self.due[kind, hop]
            for direction in (RIGHT, LEFT):
                i = self.index(direction, kind, hop)
                block = view(self.owner(direction, -hop), self.half(direction, kind))
                self.copy(block, block, direction, i).wait_recv()
                if hop < self.hops(kind):
                    self.start(block, block, direction, kind, hop + 1)

    def gather_sent(self, view):
        for direction, kind in self.each():
            block = view(self.pos, self.half(direction, kind))
            for hop in range(1, self.hops(kind) + 1):
                i = self.index(direction, kind, hop)
                self.copy(block, block, direction, i).wait_send()


class CodedRing(Ring):
    def pair(self, src, dst, direction, i):
        count = 2 * (self.n - 1)
        return self.copy(src[0], dst[0], direction, i), self.copy(src[1], dst[1], direction, count + i)

    def start_pair(self, src, dst, direction, kind, hop):
        for copy in self.pair(src, dst, direction, self.index(direction, kind, hop)):
            copy.start()
        self.due[kind, hop] = self.clock.send((self.axis, direction), self.size + 4096)

    @staticmethod
    def put(place, value):
        codes, units = encode(value)
        place[0][...] = codes
        place[1][...] = units

    @staticmethod
    def get(place):
        return decode(place[0][...], place[1][...])

    def scatter(self, view, slot, staged, after_first=None):
        for direction, kind in self.each():
            place = staged(direction * 2 + kind)
            self.put(place, view(self.owner(direction, self.hops(kind)), self.half(direction, kind)))
            self.start_pair(place, slot(self.index(direction, kind, 1)), direction, kind, 1)
            self.clock.spend(0.1)
        for kind, hop in self.events():
            yield self.due[kind, hop]
            for direction in (RIGHT, LEFT):
                i = self.index(direction, kind, hop)
                for copy in self.pair(slot(i), slot(i), direction, i):
                    copy.wait_recv()
                if hop < self.hops(kind):
                    own = view(self.owner(direction, self.hops(kind) - hop), self.half(direction, kind))
                    self.put(slot(i), self.get(slot(i)) + own)
                    self.start_pair(slot(i), slot(i + 1), direction, kind, hop + 1)
            self.clock.spend(0.4)
            if after_first is not None and (kind, hop) == (LONG, 1):
                after_first()

    def scatter_result(self, view, slot, half):
        total = view(self.pos, half)
        for direction, kind in self.each():
            if self.half(direction, kind) == half:
                total = total + self.get(slot(self.index(direction, kind, self.hops(kind))))
        return total

    def scatter_sent(self, slot):
        for direction, kind in self.each():
            for hop in range(1, self.hops(kind) + 1):
                i = self.index(direction, kind, hop)
                for copy in self.pair(slot(i), slot(i), direction, i):
                    copy.wait_send()


class Direct:
    def __init__(self, clock, size, peers, pos, owns, send_sems, recv_sems):
        self.clock, self.size, self.peers, self.pos, self.owns = clock, size, peers, pos, owns
        self.send_sems, self.recv_sems = send_sems, recv_sems

    def copy(self, src, dst, k):
        return remote(src, dst, self.send_sems(k), self.recv_sems(k), self.peers[k][0])

    def to_owners(self, action):
        same = [k for k, peer in enumerate(self.peers) if peer[2]]
        other = [k for k, peer in enumerate(self.peers) if not peer[2]]

        @pl.when(self.owns)
        def _():
            for k in same:
                action(k)

        @pl.when(jnp.logical_not(self.owns))
        def _():
            for k in other:
                action(k)

    def price(self, count):
        return max(
            self.clock.send(link, self.size * count / len(self.peers), hops) for _, _, _, link, hops in self.peers
        )

    def scatter_start(self, blocks, slots):
        self.to_owners(lambda k: self.copy(blocks.at[self.peers[k][1]], slots(k), k).start())
        return self.price(len(self.peers) // 2)

    def turn(self, blocks, slots, spread, weights, scale):
        every = range(len(self.peers))

        @pl.when(self.owns)
        def _():
            for k in every:
                self.copy(slots(k), slots(k), k).wait_recv()
            total = blocks[self.pos]
            for k in every:
                total = total + slots(k)[...]
            weights[self.pos] = softmax(total, scale)
            for k in every:
                spread.copy(weights.at[self.pos], weights.at[self.pos], k).start()

        self.clock.spend(0.6)
        return spread.price(len(self.peers) // 2)

    def arrived(self, blocks):
        self.to_owners(lambda k: self.copy(blocks.at[self.pos], blocks.at[self.pos], k).wait_recv())

    def scatter_sent(self, blocks):
        self.to_owners(lambda k: self.copy(blocks.at[self.pos], blocks.at[self.pos], k).wait_send())

    def gather_sent(self, blocks):
        @pl.when(self.owns)
        def _():
            for k in range(len(self.peers)):
                self.copy(blocks.at[self.pos], blocks.at[self.pos], k).wait_send()


def softmax(scores, scale):
    shifted = (scores - jnp.max(scores, axis=-1, keepdims=True)) * scale
    grown = jnp.exp(shifted)
    return (grown / jnp.sum(grown, axis=-1, keepdims=True)).astype(bf16)


def whole(
    scale, tok, wqkv, wo, gain, out,
    x, wq_in, wo_in, wq_t, wo_t, gain_t, qkv, att,
    s_a, s_b, s_c, r_a, r_b, r_c, acc_a, acc_b, acc_c, r_b2, r_c2, acc_b2, acc_c2, d_a, d_b, d_c,
    w_a, w_b, w_c, g_a, g_b, g_c, e_a, e_b, e_c, ue_a, ue_b, ue_c, ur_a, ur_b, ur_c, ring_sems, direct_sems,
    w_sems, x_local, x_send, x_recv, f_send, f_recv, t_send, t_recv, o_local, o_send, o_recv,
):
    y, xh, z = lax.axis_index("y"), lax.axis_index("xh"), lax.axis_index("z")
    xl, core = lax.axis_index("xl"), lax.axis_index("core")
    xpos = xh * 2 + xl

    def at_x(p):
        return {"xh": lax.div(p, 2), "xl": lax.rem(p, 2)}

    x_right, x_left = at_x(wrap(xpos + 1, NX)), at_x(wrap(xpos - 1, NX))
    y_right, y_left = {"y": wrap(y + 1, NY)}, {"y": wrap(y - 1, NY)}
    z_right, z_left = {"z": wrap(z + 1, NZ)}, {"z": wrap(z - 1, NZ)}
    plane = []
    for dx in range(NX):
        for dy in range(NY):
            if dx or dy:
                px, py = wrap(xpos + dx, NX), wrap(y + dy, NY)
                link = ("x", int(dx > NX // 2)) if dx else ("y", int(dy > NY // 2))
                far = min(dx, NX - dx) + min(dy, NY - dy)
                index = px * (NY // 2) + lax.div(py, 2)
                plane.append(({**at_x(px), "y": py}, index, (dx + dy) % 2 == 0, link, far))
    along_z = []
    for dz in range(1, NZ):
        pz = wrap(z + dz, NZ)
        along_z.append(({"z": pz}, lax.div(pz, 2), dz % 2 == 0, ("z", int(dz > NZ // 2)), min(dz, NZ - dz)))
    other_core = {"core": 1 - core}
    partner = {"xl": 1 - xl}

    loads = []
    for layer in range(LAYERS):
        for t in range(3):
            loads.append(
                pltpu.make_async_copy(
                    wqkv.at[layer, t, :, pl.ds(pl.multiple_of(core * CORE_COLS, 128), CORE_COLS)],
                    wq_in.at[layer, t],
                    w_sems.at[layer * 4 + t],
                )
            )
        loads.append(pltpu.make_async_copy(wo.at[layer], wo_in.at[layer], w_sems.at[layer * 4 + 3]))
    own_quarter, far_quarter = 2 * xl + core, 2 * (1 - xl) + core
    near_pair, far_pair = 2 * xl, 2 * (1 - xl)

    def quarter(q):
        return pl.ds(pl.multiple_of(q * QUARTER, 64), QUARTER)

    own_tokens = pltpu.make_async_copy(tok.at[pl.ds(near_pair, 2)], x.at[:, quarter(own_quarter)], x_local)
    own_tokens.start()
    for load in loads:
        load.start()

    barrier = pltpu.get_barrier_semaphore()
    partners = [peer[0] for peer in plane + along_z] + [other_core]
    for device in partners:
        pl.semaphore_signal(barrier, inc=1, device_id=device, device_id_type=MESH)
    pl.semaphore_wait(barrier, len(partners))

    def block(b):
        return slice(b * BLOCK, (b + 1) * BLOCK)

    pieces = [(b, s) for b in range(2) for s in range(2)]

    def piece(q, b, s):
        return x.at[s, quarter(q), block(b)]

    for k, (b, s) in enumerate(pieces):
        remote(
            tok.at[far_pair + s, :, block(b)], piece(own_quarter, b, s), x_send.at[k], x_recv.at[k], partner
        ).start()
    remote(
        tok.at[pl.ds(near_pair, 2)], x.at[:, quarter(own_quarter)], f_send.at[4], f_recv.at[4], other_core
    ).start()

    def turn_columns(layer, t):
        loads[layer * 4 + t].wait()
        wq_t[layer, t] = wq_in[layer, t].T

    def turn_out(layer):
        loads[layer * 4 + 3].wait()
        for m in range(3):
            wo_t[layer, m * 256 : (m + 1) * 256] = wo_in[layer, :, m * 256 : (m + 1) * 256].T
        row = gain[layer : layer + 1, :].astype(f32)
        gain_t[layer] = jnp.broadcast_to(row, (128, D)).T

    clock = Clock()

    def project(layer, t, b):
        for s in range(2):
            columns = jnp.dot(wq_t[layer, t], x[s, :, block(b)], preferred_element_type=f32)
            qkv[layer, t, :, s * HEAD_DIM : (s + 1) * HEAD_DIM, block(b)] = columns.astype(bf16).reshape(
                CORE_HEADS, HEAD_DIM, BLOCK
            )
        clock.spend(0.5)

    turn_columns(0, 0)
    turn_columns(0, 1)
    for k, (b, s) in enumerate(pieces):
        arrived = piece(far_quarter, b, s)
        remote(arrived, arrived, x_send.at[k], x_recv.at[k], partner).wait_recv()
        remote(arrived, arrived, f_send.at[k], f_recv.at[k], other_core).start()
        if k == 0:
            turn_columns(0, 2)
            own_tokens.wait()
            near = x.at[:, quarter(2 * xl + 1 - core)]
            remote(near, near, f_send.at[4], f_recv.at[4], other_core).wait_recv()
        if k == 2:
            for j in range(2):
                arrived = piece(2 * (1 - xl) + 1 - core, *pieces[j])
                remote(arrived, arrived, f_send.at[j], f_recv.at[j], other_core).wait_recv()
            project(0, 0, 0)
            project(0, 1, 0)
    for j in range(2, 4):
        arrived = piece(2 * (1 - xl) + 1 - core, *pieces[j])
        remote(arrived, arrived, f_send.at[j], f_recv.at[j], other_core).wait_recv()
    project(0, 0, 1)
    project(0, 1, 1)

    def tokens_sent():
        for k, (b, s) in enumerate(pieces):
            arrived = piece(far_quarter, b, s)
            remote(arrived, arrived, x_send.at[k], x_recv.at[k], partner).wait_send()
            remote(arrived, arrived, f_send.at[k], f_recv.at[k], other_core).wait_send()
        near = x.at[:, quarter(own_quarter)]
        remote(near, near, f_send.at[4], f_recv.at[4], other_core).wait_send()

    plane_pos = xpos * (NY // 2) + lax.div(y, 2)
    z_pos = lax.div(z, 2)
    plane_parity, z_parity = lax.rem(xpos + y, 2), lax.rem(z, 2)

    def taker(table):
        taken = [0]

        def take(count):
            first = taken[0]
            taken[0] += count
            return lambda i: table.at[first + i]

        return take

    row = RES * 4

    def colour_rings(b):
        take_ring, take_direct = taker(ring_sems.at[b]), taker(direct_sems.at[b])

        def ring(axis, rows, width, kind=Ring):
            n, pos, right, left = {
                "x": (NX, xpos, x_right, x_left),
                "y": (NY, y, y_right, y_left),
                "z": (NZ, z, z_right, z_left),
            }[axis]
            count = 2 * (n - 1) * (2 if kind is CodedRing else 1)
            return kind(clock, axis, rows * row * width, n, pos, right, left, take_ring(count), take_ring(count))

        def direct(peers, width):
            pos, parity = (plane_pos, plane_parity) if peers is plane else (z_pos, z_parity)
            return Direct(
                clock, 8 * row * width, peers, pos, parity == b, take_direct(len(peers)), take_direct(len(peers))
            )

        return [
            dict(
                down=[ring("z", 32, 0.5, CodedRing)], owners=direct(plane, 1), spread=direct(plane, 0.5), up=[ring("z", 32, 0.5)]
            )
        ] + [
            dict(
                down=[ring(first, 64, 0.5, CodedRing), ring(second, 16, 1)],
                owners=direct(along_z, 1),
                spread=direct(along_z, 0.5),
                up=[ring(second, 16, 0.5), ring(first, 64, 0.5)],
            )
            for first, second in (("y", "x"), ("x", "y"))
        ]

    groups = [colour_rings(b) for b in range(2)]

    def slots(ref, b):
        return lambda i: ref.at[b, i]

    def pairs(ref, b):
        return lambda owner, half: ref.at[b, 2 * owner + half]

    def fours(ref, b):
        return lambda owner, half: ref.at[b, owner, pl.ds(4 * half, 4)]

    def coded(codes, units, b):
        return lambda i: (codes.at[b, i], units.at[b, i])

    def terms(view):
        return lambda owner, half: view(owner, half)[...].reshape(-1, RES)

    places = [
        dict(s=s_a, r=(r_a, ur_a), e=(e_a, ue_a), r2=None, acc=None, last=acc_a, d=d_a, w=w_a, g=g_a, view=pairs, blocks=(8, 32)),
        dict(s=s_b, r=(r_b, ur_b), e=(e_b, ue_b), r2=r_b2, acc=acc_b, last=acc_b2, d=d_b, w=w_b, g=g_b, view=fours, blocks=(2, 8, 16)),
        dict(s=s_c, r=(r_c, ur_c), e=(e_c, ue_c), r2=r_c2, acc=acc_c, last=acc_c2, d=d_c, w=w_c, g=g_c, view=fours, blocks=(2, 8, 16)),
    ]
    middle = [None, lambda b: lambda owner, half: w_b.at[b, y, 2 * owner + half],
              lambda b: lambda owner, half: w_c.at[b, xpos, 2 * owner + half]]

    def trade(layer, b, colour, owner):
        part = att.at[layer, :, owner, pl.ds(128 * colour, 128), block(b)]
        return remote(part, part, t_send.at[b, colour], t_recv.at[layer, b, colour], other_core)

    def score(layer, b, colour):
        place = places[colour]
        blocks = place["blocks"]

        def body(h, carry):
            head = 2 * colour + h
            scores = jnp.dot(
                qkv[layer, 0, head, :, block(b)].T, qkv[layer, 1, head], preferred_element_type=f32
            )
            place["s"][b, pl.ds(h * blocks[0], blocks[0])] = scores.reshape(*blocks, RES)
            return carry

        lax.fori_loop(0, 2, body, 0)
        clock.spend(0.5)

    def attend(layer, b, colour):
        place = places[colour]
        blocks = place["blocks"]

        def body(h, carry):
            head = 2 * colour + h
            weights = place["w"][b, pl.ds(h * blocks[0], blocks[0])].reshape(BLOCK, RES)
            heads = lax.dot_general(
                qkv[layer, 2, head], weights, (((1,), (1,)), ((), ())), preferred_element_type=f32
            ).astype(bf16)
            at = pl.ds(pl.multiple_of(head * HEAD_DIM, HEAD_DIM), HEAD_DIM)
            for s in range(2):
                att[layer, s, core, at, block(b)] = heads[s * HEAD_DIM : (s + 1) * HEAD_DIM]
            return carry

        lax.fori_loop(0, 2, body, 0)
        clock.spend(0.6)

    def joined(ref, b, first, blocks):
        return ref[b, first : first + blocks].astype(f32).reshape(blocks * 8, RES).astype(bf16)

    def colour_steps(layer, b, colour, after_first, done):
        place, group = places[colour], groups[b][colour]
        view, slot, staged = terms(place["view"](place["s"], b)), coded(*place["r"], b), coded(*place["e"], b)
        score(layer, b, colour)
        down = group["down"]
        yield from down[0].scatter(view, slot, staged, after_first)
        last = place["last"].at[b]
        if colour == 0:
            for half in range(2):
                last[4 * half : 4 * half + 4] = down[0].scatter_result(view, slot, half).reshape(4, 8, RES)
        else:
            view2, slot2 = pairs(place["acc"], b), slots(place["r2"], b)
            for half in range(2):
                place["acc"][b, 4 * half : 4 * half + 4] = down[0].scatter_result(view, slot, half).reshape(4, 16, RES)
            yield from down[1].scatter(view2, slot2)
            for half in range(2):
                last[2 * half : 2 * half + 2] = down[1].scatter_result(view2, slot2, half).reshape(2, 8, RES)
            down[1].scatter_sent(slot2)
        down[0].scatter_sent(slot)
        yield group["owners"].scatter_start(last, slots(place["d"], b))
        yield group["owners"].turn(last, slots(place["d"], b), group["spread"], place["g"].at[b], scale)
        group["spread"].arrived(place["g"].at[b])
        w, up = place["w"], group["up"]
        if colour == 0:
            for half in range(2):
                w[b, 2 * z + half] = joined(place["g"], b, 4 * half, 4)
        else:
            first, second = (y, xpos) if colour == 1 else (xpos, y)
            for half in range(2):
                w[b, first, 2 * second + half] = joined(place["g"], b, 2 * half, 2)
            yield from up[0].gather(middle[colour](b))
        yield from up[-1].gather(place["view"](w, b))
        attend(layer, b, colour)
        trade(layer, b, colour, core).start()
        done()

    def all_sent(b):
        for colour in range(3):
            place, group = places[colour], groups[b][colour]
            group["owners"].scatter_sent(place["last"].at[b])
            group["spread"].gather_sent(place["g"].at[b])
            group["up"][-1].gather_sent(place["view"](place["w"], b))
            if colour:
                group["up"][0].gather_sent(middle[colour](b))

    def finish(layer, b):
        def body(s, carry):
            heads = att[layer, s, :, :, block(b)].reshape(D, BLOCK)
            update = jnp.dot(wo_t[layer], heads, preferred_element_type=f32)
            summed = x[s, :, block(b)].astype(f32) + update
            mean_sq = jnp.mean(summed * summed, axis=0, keepdims=True)
            gains = gain_t[layer]
            normed = summed * lax.rsqrt(mean_sq + EPSILON) * jnp.concatenate([gains, gains], axis=1)
            x[s, :, block(b)] = normed.astype(bf16)
            return carry

        lax.fori_loop(0, 2, body, 0)
        clock.spend(1.5)

    def far_out(b):
        return remote(
            x.at[:, quarter(far_quarter), block(b)], out.at[pl.ds(near_pair, 2), :, block(b)],
            o_send.at[b], o_recv.at[b], partner,
        )

    def own_out(b):
        return pltpu.make_async_copy(
            x.at[:, quarter(own_quarter), block(b)], out.at[pl.ds(near_pair, 2), :, block(b)], o_local.at[b]
        )

    def finish_steps(layer, b):
        yield clock.now + 1.6
        for colour in range(3):
            trade(layer, b, colour, 1 - core).wait_recv()
        finish(layer, b)
        if layer + 1 < LAYERS:
            project(layer + 1, 0, b)
            project(layer + 1, 1, b)
        else:
            far_out(b).start()
            own_out(b).start()

    for layer in range(LAYERS):
        running, order = [], [0]

        def add(steps, running=running, order=order):
            due = next(steps, None)
            if due is not None:
                order[0] += 1
                running.append((due, order[0], steps))

        def launch(b, colour, layer=layer, add=add):
            left[b][colour] = 1

            def after_first():
                if b == 0:
                    launch(1, colour)

            def done():
                left[b][colour] = 0
                if sum(left[b].values()) == 0 and len(left[b]) == 3:
                    add(finish_steps(layer, b))

            add(colour_steps(layer, b, colour, after_first, done))

        left = [{}, {}]
        for colour in range(3):
            launch(0, colour)
        for b in range(2):
            project(layer, 2, b)
        fillers = []
        if layer == 0:
            tokens_sent()
            fillers = [functools.partial(turn_out, 0)]
            fillers += [functools.partial(turn_columns, 1, t) for t in range(3)]
            fillers += [functools.partial(turn_out, 1)]
        while running:
            running.sort(key=lambda entry: entry[:2])
            if fillers and running[0][0] > clock.now + 0.7:
                fillers.pop(0)()
                clock.spend(1.0)
                continue
            due, _, steps = running.pop(0)
            clock.now = max(clock.now, due)
            add(steps)
        for filler in fillers:
            filler()
        for b in range(2):
            all_sent(b)
            for colour in range(3):
                trade(layer, b, colour, core).wait_send()

    for b in range(2):
        own_out(b).wait()
        far_out(b).wait_send()
        landed = out.at[pl.ds(far_pair, 2), :, block(b)]
        remote(landed, landed, o_send.at[b], o_recv.at[b], partner).wait_recv()


def on_device(tokens, qkv_weight, out_weight, norm_gain):
    scale = 1.0 / (HEAD_DIM * 2 * NX * NY * NZ) ** 0.5
    any_space = pl.BlockSpec(memory_space=pl.ANY)
    vmem = pl.BlockSpec(memory_space=pltpu.VMEM)
    dma = pltpu.SemaphoreType.DMA
    around = lambda n: 2 * (n - 1)
    ring_count = 4 * (around(NZ) + 2 * around(NX) + 2 * around(NY)) + 2 * (around(NZ) + around(NX) + around(NY))
    direct_count = 4 * (NX * NY - 1 + 2 * (NZ - 1))
    result = pl.pallas_call(
        functools.partial(whole, scale),
        out_shape=jax.ShapeDtypeStruct((4, QUARTER, RES), bf16),
        in_specs=[any_space, any_space, any_space, vmem],
        out_specs=any_space,
        scratch_shapes=[
            pltpu.VMEM((2, D, RES), bf16),
            pltpu.VMEM((LAYERS, 3, D, CORE_COLS), bf16),
            pltpu.VMEM((LAYERS, D, D), bf16),
            pltpu.VMEM((LAYERS, 3, CORE_COLS, D), bf16),
            pltpu.VMEM((LAYERS, D, D), bf16),
            pltpu.VMEM((LAYERS, D, 128), f32),
            pltpu.VMEM((LAYERS, 3, CORE_HEADS, 2 * HEAD_DIM, RES), bf16),
            pltpu.VMEM((LAYERS, 2, 2, CORE_COLS, RES), bf16),
            pltpu.VMEM((2, 16, 32, RES), f32),
            pltpu.VMEM((2, 4, 8, 16, RES), f32),
            pltpu.VMEM((2, 4, 8, 16, RES), f32),
            pltpu.VMEM((2, 14, 32, RES), bf16),
            pltpu.VMEM((2, 6, 64, RES), bf16),
            pltpu.VMEM((2, 6, 64, RES), bf16),
            pltpu.VMEM((2, 8, 8, RES), f32),
            pltpu.VMEM((2, 8, 16, RES), f32),
            pltpu.VMEM((2, 8, 16, RES), f32),
            pltpu.VMEM((2, 6, 16, RES), f32),
            pltpu.VMEM((2, 6, 16, RES), f32),
            pltpu.VMEM((2, 4, 8, RES), f32),
            pltpu.VMEM((2, 4, 8, RES), f32),
            pltpu.VMEM((2, 15, 8, RES), f32),
            pltpu.VMEM((2, 7, 8, RES), f32),
            pltpu.VMEM((2, 7, 8, RES), f32),
            pltpu.VMEM((2, 16, 32, RES), bf16),
            pltpu.VMEM((2, 4, 8, 16, RES), bf16),
            pltpu.VMEM((2, 4, 8, 16, RES), bf16),
            pltpu.VMEM((2, 8, 8, RES), bf16),
            pltpu.VMEM((2, 4, 8, RES), bf16),
            pltpu.VMEM((2, 4, 8, RES), bf16),
            pltpu.VMEM((2, 4, 32, RES), bf16),
            pltpu.VMEM((2, 4, 64, RES), bf16),
            pltpu.VMEM((2, 4, 64, RES), bf16),
            pltpu.VMEM((2, 4, 8, 128), f32),
            pltpu.VMEM((2, 4, 8, 128), f32),
            pltpu.VMEM((2, 4, 8, 128), f32),
            pltpu.VMEM((2, 14, 8, 128), f32),
            pltpu.VMEM((2, 6, 8, 128), f32),
            pltpu.VMEM((2, 6, 8, 128), f32),
            dma((2, ring_count)),
            dma((2, direct_count)),
            dma((4 * LAYERS,)),
            dma,
            dma((4,)),
            dma((4,)),
            dma((5,)),
            dma((5,)),
            dma((2, 3)),
            dma((LAYERS, 2, 3)),
            dma((2,)),
            dma((2,)),
            dma((2,)),
        ],
        compiler_params=pltpu.CompilerParams(
            collective_id=0, has_side_effects=True, vmem_limit_bytes=60 * 1024 * 1024
        ),
    )(
        tokens.transpose(0, 2, 1),
        qkv_weight.transpose(0, 2, 1, 3),
        out_weight,
        norm_gain,
    )
    return result.transpose(0, 2, 1)


def solution(mesh):
    finer = Mesh(mesh.devices.reshape(NY, NX // 2, NZ, 2, 2), AXES)
    rows, heads = ("y", "xh", "z"), ("xl", "core")
    return jax.shard_map(
        on_device,
        mesh=finer,
        in_specs=(P(rows, None, heads), P(), P(), P()),
        out_specs=P(rows, None, heads),
        check_vma=False,
    )
```

```python
import functools

import jax
import jax.numpy as jnp
from jax import lax
from jax.experimental import pallas as pl
from jax.experimental.pallas import tpu as pltpu
from jax.sharding import Mesh
from jax.sharding import PartitionSpec as P

D = 768
HEADS = 12
HEAD_DIM = 64
LAYERS = 2
EPSILON = 1e-06
MESH = pl.DeviceIdType.MESH
AXES = ("y", "xh", "z", "xl", "core")
NX, NY, NZ = 4, 4, 8
RES = 512
BLOCK = RES // 2
CORE_HEADS = HEADS // 2
CORE_COLS = CORE_HEADS * HEAD_DIM
QUARTER = D // 4
f32, bf16 = jnp.float32, jnp.bfloat16

RIGHT, LEFT = 0, 1
LONG, SHORT = 0, 1


def wrap(value, n):
    return lax.rem(value + 2 * n, n)


def remote(src, dst, send_sem, recv_sem, device):
    return pltpu.make_async_remote_copy(
        src_ref=src, dst_ref=dst, send_sem=send_sem, recv_sem=recv_sem, device_id=device, device_id_type=MESH
    )


STEPS = 195.0
LOWEST = 100.0


def encode(value):
    rows, columns = value.shape
    size = jnp.abs(value)
    top = functools.reduce(
        jnp.maximum,
        [size[r : r + 8, c : c + 128] for r in range(0, rows, 8) for c in range(0, columns, 128)],
    )
    top = jnp.maximum(top, 1e-30)
    per_unit = jnp.concatenate([STEPS / top] * (columns // 128), axis=1)
    per_unit = jnp.concatenate([per_unit] * (rows // 8), axis=0)
    level = size * per_unit
    binade = jnp.floor(level)
    code = (1.0 + (level - binade)) * jnp.exp2(binade - LOWEST)
    return jnp.where(value < 0, -code, code).astype(bf16), top / STEPS


def decode(code, unit):
    rows, columns = code.shape
    code = code.astype(f32)
    size = jnp.abs(code)
    binade = jnp.floor(jnp.log2(size))
    level = binade + size * jnp.exp2(-binade) + (LOWEST - 1.0)
    unit = jnp.concatenate([unit] * (columns // 128), axis=1)
    unit = jnp.concatenate([unit] * (rows // 8), axis=0)
    return jnp.where(code < 0, -level, level) * unit


class Clock:
    RATE, FIRST_HOP, NEXT_HOP = 46e3, 3.0, 0.65

    def __init__(self):
        self.now, self.free = 0.0, {}

    def spend(self, time):
        self.now += time

    def send(self, link, size, hops=1):
        begin = max(self.now, self.free.get(link, 0.0))
        self.free[link] = begin + size / self.RATE
        return self.free[link] + self.FIRST_HOP + self.NEXT_HOP * (hops - 1)


class Ring:
    def __init__(self, clock, axis, size, n, pos, right, left, send_sems, recv_sems):
        self.clock, self.axis, self.size = clock, axis, size
        self.n, self.pos, self.devices = n, pos, (right, left)
        self.send_sems, self.recv_sems = send_sems, recv_sems
        self.due = {}

    def hops(self, kind):
        return self.n // 2 - kind

    def half(self, direction, kind):
        return direction ^ kind

    def index(self, direction, kind, hop):
        return direction * (self.n - 1) + kind * (self.n // 2) + hop - 1

    def owner(self, direction, distance):
        return wrap(self.pos + (distance if direction == RIGHT else -distance), self.n)

    def copy(self, src, dst, direction, i):
        return remote(src, dst, self.send_sems(i), self.recv_sems(i), self.devices[direction])

    def start(self, src, dst, direction, kind, hop):
        self.copy(src, dst, direction, self.index(direction, kind, hop)).start()
        self.due[kind, hop] = self.clock.send((self.axis, direction), self.size)

    def each(self):
        for kind in (LONG, SHORT):
            for direction in (RIGHT, LEFT):
                yield direction, kind

    def events(self):
        for hop in range(1, self.n // 2 + 1):
            for kind in (LONG, SHORT):
                if hop <= self.hops(kind):
                    yield kind, hop

    def scatter(self, view, slot):
        for direction, kind in self.each():
            own = view(self.owner(direction, self.hops(kind)), self.half(direction, kind))
            self.start(own, slot(self.index(direction, kind, 1)), direction, kind, 1)
        for kind, hop in self.events():
            yield self.due[kind, hop]
            for direction in (RIGHT, LEFT):
                i = self.index(direction, kind, hop)
                self.copy(slot(i), slot(i), direction, i).wait_recv()
                if hop < self.hops(kind):
                    own = view(self.owner(direction, self.hops(kind) - hop), self.half(direction, kind))
                    slot(i)[...] = slot(i)[...] + own[...]
                    self.start(slot(i), slot(i + 1), direction, kind, hop + 1)
            self.clock.spend(self.size / 500e3)

    def scatter_result(self, view, slot, half):
        total = view(self.pos, half)[...]
        for direction, kind in self.each():
            if self.half(direction, kind) == half:
                total = total + slot(self.index(direction, kind, self.hops(kind)))[...]
        return total

    def scatter_sent(self, slot):
        for direction, kind in self.each():
            for hop in range(1, self.hops(kind) + 1):
                i = self.index(direction, kind, hop)
                self.copy(slot(i), slot(i), direction, i).wait_send()

    def gather(self, view):
        for direction, kind in self.each():
            block = view(self.pos, self.half(direction, kind))
            self.start(block, block, direction, kind, 1)
        for kind, hop in self.events():
            yield self.due[kind, hop]
            for direction in (RIGHT, LEFT):
                i = self.index(direction, kind, hop)
                block = view(self.owner(direction, -hop), self.half(direction, kind))
                self.copy(block, block, direction, i).wait_recv()
                if hop < self.hops(kind):
                    self.start(block, block, direction, kind, hop + 1)

    def gather_sent(self, view):
        for direction, kind in self.each():
            block = view(self.pos, self.half(direction, kind))
            for hop in range(1, self.hops(kind) + 1):
                i = self.index(direction, kind, hop)
                self.copy(block, block, direction, i).wait_send()


class CodedRing(Ring):
    def pair(self, src, dst, direction, i):
        count = 2 * (self.n - 1)
        return self.copy(src[0], dst[0], direction, i), self.copy(src[1], dst[1], direction, count + i)

    def start_pair(self, src, dst, direction, kind, hop):
        for copy in self.pair(src, dst, direction, self.index(direction, kind, hop)):
            copy.start()
        self.due[kind, hop] = self.clock.send((self.axis, direction), self.size + 4096)

    @staticmethod
    def put(place, value):
        codes, units = encode(value)
        place[0][...] = codes
        place[1][...] = units

    @staticmethod
    def get(place):
        return decode(place[0][...], place[1][...])

    def scatter(self, view, slot, staged):
        for direction, kind in self.each():
            place = staged(direction * 2 + kind)
            self.put(place, view(self.owner(direction, self.hops(kind)), self.half(direction, kind)))
            self.start_pair(place, slot(self.index(direction, kind, 1)), direction, kind, 1)
            self.clock.spend(0.1)
        for kind, hop in self.events():
            yield self.due[kind, hop]
            for direction in (RIGHT, LEFT):
                i = self.index(direction, kind, hop)
                for copy in self.pair(slot(i), slot(i), direction, i):
                    copy.wait_recv()
                if hop < self.hops(kind):
                    own = view(self.owner(direction, self.hops(kind) - hop), self.half(direction, kind))
                    self.put(slot(i), self.get(slot(i)) + own)
                    self.start_pair(slot(i), slot(i + 1), direction, kind, hop + 1)
            self.clock.spend(0.4)

    def scatter_result(self, view, slot, half):
        total = view(self.pos, half)
        for direction, kind in self.each():
            if self.half(direction, kind) == half:
                total = total + self.get(slot(self.index(direction, kind, self.hops(kind))))
        return total

    def scatter_sent(self, slot):
        for direction, kind in self.each():
            for hop in range(1, self.hops(kind) + 1):
                i = self.index(direction, kind, hop)
                for copy in self.pair(slot(i), slot(i), direction, i):
                    copy.wait_send()


class Direct:
    def __init__(self, clock, size, peers, pos, owns, send_sems, recv_sems):
        self.clock, self.size, self.peers, self.pos, self.owns = clock, size, peers, pos, owns
        self.send_sems, self.recv_sems = send_sems, recv_sems

    def copy(self, src, dst, k):
        return remote(src, dst, self.send_sems(k), self.recv_sems(k), self.peers[k][0])

    def to_owners(self, action):
        same = [k for k, peer in enumerate(self.peers) if peer[2]]
        other = [k for k, peer in enumerate(self.peers) if not peer[2]]

        @pl.when(self.owns)
        def _():
            for k in same:
                action(k)

        @pl.when(jnp.logical_not(self.owns))
        def _():
            for k in other:
                action(k)

    def price(self, count):
        return max(
            self.clock.send(link, self.size * count / len(self.peers), hops) for _, _, _, link, hops in self.peers
        )

    def scatter_start(self, blocks, slots):
        self.to_owners(lambda k: self.copy(blocks.at[self.peers[k][1]], slots(k), k).start())
        return self.price(len(self.peers) // 2)

    def turn(self, blocks, slots, spread, weights, scale):
        every = range(len(self.peers))

        @pl.when(self.owns)
        def _():
            for k in every:
                self.copy(slots(k), slots(k), k).wait_recv()
            total = blocks[self.pos]
            for k in every:
                total = total + slots(k)[...]
            weights[self.pos] = softmax(total, scale)
            for k in every:
                spread.copy(weights.at[self.pos], weights.at[self.pos], k).start()

        self.clock.spend(0.6)
        return spread.price(len(self.peers) // 2)

    def arrived(self, blocks):
        self.to_owners(lambda k: self.copy(blocks.at[self.pos], blocks.at[self.pos], k).wait_recv())

    def scatter_sent(self, blocks):
        self.to_owners(lambda k: self.copy(blocks.at[self.pos], blocks.at[self.pos], k).wait_send())

    def gather_sent(self, blocks):
        @pl.when(self.owns)
        def _():
            for k in range(len(self.peers)):
                self.copy(blocks.at[self.pos], blocks.at[self.pos], k).wait_send()


def softmax(scores, scale):
    shifted = (scores - jnp.max(scores, axis=-1, keepdims=True)) * scale
    grown = jnp.exp(shifted)
    return (grown / jnp.sum(grown, axis=-1, keepdims=True)).astype(bf16)


def whole(
    scale, tok, wqkv, wo, gain, out,
    x, wq_in, wo_in, wq_t, wo_t, gain_t, qkv, att,
    s_a, s_b, s_c, r_a, r_b, r_c, acc_a, acc_b, acc_c, r_b2, r_c2, acc_b2, acc_c2, d_a, d_b, d_c,
    w_a, w_b, w_c, g_a, g_b, g_c, e_a, e_b, e_c, ue_a, ue_b, ue_c, ur_a, ur_b, ur_c, ring_sems, direct_sems,
    w_sems, x_local, x_send, x_recv, f_send, f_recv, t_send, t_recv, o_local, o_send, o_recv,
):
    y, xh, z = lax.axis_index("y"), lax.axis_index("xh"), lax.axis_index("z")
    xl, core = lax.axis_index("xl"), lax.axis_index("core")
    xpos = xh * 2 + xl

    def at_x(p):
        return {"xh": lax.div(p, 2), "xl": lax.rem(p, 2)}

    x_right, x_left = at_x(wrap(xpos + 1, NX)), at_x(wrap(xpos - 1, NX))
    y_right, y_left = {"y": wrap(y + 1, NY)}, {"y": wrap(y - 1, NY)}
    z_right, z_left = {"z": wrap(z + 1, NZ)}, {"z": wrap(z - 1, NZ)}
    plane = []
    for dx in range(NX):
        for dy in range(NY):
            if dx or dy:
                px, py = wrap(xpos + dx, NX), wrap(y + dy, NY)
                link = ("x", int(dx > NX // 2)) if dx else ("y", int(dy > NY // 2))
                far = min(dx, NX - dx) + min(dy, NY - dy)
                index = px * (NY // 2) + lax.div(py, 2)
                plane.append(({**at_x(px), "y": py}, index, (dx + dy) % 2 == 0, link, far))
    along_z = []
    for dz in range(1, NZ):
        pz = wrap(z + dz, NZ)
        along_z.append(({"z": pz}, lax.div(pz, 2), dz % 2 == 0, ("z", int(dz > NZ // 2)), min(dz, NZ - dz)))
    other_core = {"core": 1 - core}
    partner = {"xl": 1 - xl}

    loads = []
    for layer in range(LAYERS):
        for t in range(3):
            loads.append(
                pltpu.make_async_copy(
                    wqkv.at[layer, t, :, pl.ds(pl.multiple_of(core * CORE_COLS, 128), CORE_COLS)],
                    wq_in.at[layer, t],
                    w_sems.at[layer * 4 + t],
                )
            )
        loads.append(pltpu.make_async_copy(wo.at[layer], wo_in.at[layer], w_sems.at[layer * 4 + 3]))
    own_quarter, far_quarter = 2 * xl + core, 2 * (1 - xl) + core
    near_pair, far_pair = 2 * xl, 2 * (1 - xl)

    def quarter(q):
        return pl.ds(pl.multiple_of(q * QUARTER, 64), QUARTER)

    own_tokens = pltpu.make_async_copy(tok.at[pl.ds(near_pair, 2)], x.at[:, quarter(own_quarter)], x_local)
    own_tokens.start()
    for load in loads:
        load.start()

    barrier = pltpu.get_barrier_semaphore()
    partners = [peer[0] for peer in plane + along_z] + [other_core]
    for device in partners:
        pl.semaphore_signal(barrier, inc=1, device_id=device, device_id_type=MESH)
    pl.semaphore_wait(barrier, len(partners))

    def block(b):
        return slice(b * BLOCK, (b + 1) * BLOCK)

    pieces = [(b, s) for b in range(2) for s in range(2)]

    def piece(q, b, s):
        return x.at[s, quarter(q), block(b)]

    for k, (b, s) in enumerate(pieces):
        remote(
            tok.at[far_pair + s, :, block(b)], piece(own_quarter, b, s), x_send.at[k], x_recv.at[k], partner
        ).start()
    remote(
        tok.at[pl.ds(near_pair, 2)], x.at[:, quarter(own_quarter)], f_send.at[4], f_recv.at[4], other_core
    ).start()

    def turn_columns(layer, t):
        loads[layer * 4 + t].wait()
        wq_t[layer, t] = wq_in[layer, t].T

    def turn_out(layer):
        loads[layer * 4 + 3].wait()
        for m in range(3):
            wo_t[layer, m * 256 : (m + 1) * 256] = wo_in[layer, :, m * 256 : (m + 1) * 256].T
        row = gain[layer : layer + 1, :].astype(f32)
        gain_t[layer] = jnp.broadcast_to(row, (128, D)).T

    clock = Clock()

    def project(layer, t, b):
        for s in range(2):
            columns = jnp.dot(wq_t[layer, t], x[s, :, block(b)], preferred_element_type=f32)
            qkv[layer, t, :, s * HEAD_DIM : (s + 1) * HEAD_DIM, block(b)] = columns.astype(bf16).reshape(
                CORE_HEADS, HEAD_DIM, BLOCK
            )
        clock.spend(0.5)

    turn_columns(0, 0)
    turn_columns(0, 1)
    for k, (b, s) in enumerate(pieces):
        arrived = piece(far_quarter, b, s)
        remote(arrived, arrived, x_send.at[k], x_recv.at[k], partner).wait_recv()
        remote(arrived, arrived, f_send.at[k], f_recv.at[k], other_core).start()
        if k == 0:
            turn_columns(0, 2)
            own_tokens.wait()
            near = x.at[:, quarter(2 * xl + 1 - core)]
            remote(near, near, f_send.at[4], f_recv.at[4], other_core).wait_recv()
        if k == 2:
            for j in range(2):
                arrived = piece(2 * (1 - xl) + 1 - core, *pieces[j])
                remote(arrived, arrived, f_send.at[j], f_recv.at[j], other_core).wait_recv()
            project(0, 0, 0)
            project(0, 1, 0)
    for j in range(2, 4):
        arrived = piece(2 * (1 - xl) + 1 - core, *pieces[j])
        remote(arrived, arrived, f_send.at[j], f_recv.at[j], other_core).wait_recv()
    project(0, 0, 1)
    project(0, 1, 1)

    def tokens_sent():
        for k, (b, s) in enumerate(pieces):
            arrived = piece(far_quarter, b, s)
            remote(arrived, arrived, x_send.at[k], x_recv.at[k], partner).wait_send()
            remote(arrived, arrived, f_send.at[k], f_recv.at[k], other_core).wait_send()
        near = x.at[:, quarter(own_quarter)]
        remote(near, near, f_send.at[4], f_recv.at[4], other_core).wait_send()

    plane_pos = xpos * (NY // 2) + lax.div(y, 2)
    z_pos = lax.div(z, 2)
    plane_parity, z_parity = lax.rem(xpos + y, 2), lax.rem(z, 2)

    def taker(table):
        taken = [0]

        def take(count):
            first = taken[0]
            taken[0] += count
            return lambda i: table.at[first + i]

        return take

    row = RES * 4

    def colour_rings(b):
        take_ring, take_direct = taker(ring_sems.at[b]), taker(direct_sems.at[b])

        def ring(axis, rows, width, kind=Ring):
            n, pos, right, left = {
                "x": (NX, xpos, x_right, x_left),
                "y": (NY, y, y_right, y_left),
                "z": (NZ, z, z_right, z_left),
            }[axis]
            count = 2 * (n - 1) * (2 if kind is CodedRing else 1)
            return kind(clock, axis, rows * row * width, n, pos, right, left, take_ring(count), take_ring(count))

        def direct(peers, width):
            pos, parity = (plane_pos, plane_parity) if peers is plane else (z_pos, z_parity)
            return Direct(
                clock, 8 * row * width, peers, pos, parity == b, take_direct(len(peers)), take_direct(len(peers))
            )

        return [
            dict(
                down=[ring("z", 32, 0.5, CodedRing)], owners=direct(plane, 1), spread=direct(plane, 0.5), up=[ring("z", 32, 0.5)]
            )
        ] + [
            dict(
                down=[ring(first, 64, 0.5, CodedRing), ring(second, 16, 1)],
                owners=direct(along_z, 1),
                spread=direct(along_z, 0.5),
                up=[ring(second, 16, 0.5), ring(first, 64, 0.5)],
            )
            for first, second in (("y", "x"), ("x", "y"))
        ]

    groups = [colour_rings(b) for b in range(2)]

    def slots(ref, b):
        return lambda i: ref.at[b, i]

    def pairs(ref, b):
        return lambda owner, half: ref.at[b, 2 * owner + half]

    def fours(ref, b):
        return lambda owner, half: ref.at[b, owner, pl.ds(4 * half, 4)]

    def coded(codes, units, b):
        return lambda i: (codes.at[b, i], units.at[b, i])

    def terms(view):
        return lambda owner, half: view(owner, half)[...].reshape(-1, RES)

    places = [
        dict(s=s_a, r=(r_a, ur_a), e=(e_a, ue_a), r2=None, acc=None, last=acc_a, d=d_a, w=w_a, g=g_a, view=pairs, blocks=(8, 32)),
        dict(s=s_b, r=(r_b, ur_b), e=(e_b, ue_b), r2=r_b2, acc=acc_b, last=acc_b2, d=d_b, w=w_b, g=g_b, view=fours, blocks=(2, 8, 16)),
        dict(s=s_c, r=(r_c, ur_c), e=(e_c, ue_c), r2=r_c2, acc=acc_c, last=acc_c2, d=d_c, w=w_c, g=g_c, view=fours, blocks=(2, 8, 16)),
    ]
    middle = [None, lambda b: lambda owner, half: w_b.at[b, y, 2 * owner + half],
              lambda b: lambda owner, half: w_c.at[b, xpos, 2 * owner + half]]

    def trade(layer, b, colour, owner):
        part = att.at[layer, :, owner, pl.ds(128 * colour, 128), block(b)]
        return remote(part, part, t_send.at[b, colour], t_recv.at[layer, b, colour], other_core)

    def score(layer, b, colour):
        place = places[colour]
        blocks = place["blocks"]

        def body(h, carry):
            head = 2 * colour + h
            scores = jnp.dot(
                qkv[layer, 0, head, :, block(b)].T, qkv[layer, 1, head], preferred_element_type=f32
            )
            place["s"][b, pl.ds(h * blocks[0], blocks[0])] = scores.reshape(*blocks, RES)
            return carry

        lax.fori_loop(0, 2, body, 0)
        clock.spend(0.5)

    def attend(layer, b, colour):
        place = places[colour]
        blocks = place["blocks"]

        def body(h, carry):
            head = 2 * colour + h
            weights = place["w"][b, pl.ds(h * blocks[0], blocks[0])].reshape(BLOCK, RES)
            heads = lax.dot_general(
                qkv[layer, 2, head], weights, (((1,), (1,)), ((), ())), preferred_element_type=f32
            ).astype(bf16)
            at = pl.ds(pl.multiple_of(head * HEAD_DIM, HEAD_DIM), HEAD_DIM)
            for s in range(2):
                att[layer, s, core, at, block(b)] = heads[s * HEAD_DIM : (s + 1) * HEAD_DIM]
            return carry

        lax.fori_loop(0, 2, body, 0)
        clock.spend(0.6)

    def joined(ref, b, first, blocks):
        return ref[b, first : first + blocks].astype(f32).reshape(blocks * 8, RES).astype(bf16)

    def colour_steps(layer, b, colour, done):
        place, group = places[colour], groups[b][colour]
        view, slot, staged = terms(place["view"](place["s"], b)), coded(*place["r"], b), coded(*place["e"], b)
        score(layer, b, colour)
        down = group["down"]
        yield from down[0].scatter(view, slot, staged)
        last = place["last"].at[b]
        if colour == 0:
            for half in range(2):
                last[4 * half : 4 * half + 4] = down[0].scatter_result(view, slot, half).reshape(4, 8, RES)
        else:
            view2, slot2 = pairs(place["acc"], b), slots(place["r2"], b)
            for half in range(2):
                place["acc"][b, 4 * half : 4 * half + 4] = down[0].scatter_result(view, slot, half).reshape(4, 16, RES)
            yield from down[1].scatter(view2, slot2)
            for half in range(2):
                last[2 * half : 2 * half + 2] = down[1].scatter_result(view2, slot2, half).reshape(2, 8, RES)
            down[1].scatter_sent(slot2)
        down[0].scatter_sent(slot)
        yield group["owners"].scatter_start(last, slots(place["d"], b))
        yield group["owners"].turn(last, slots(place["d"], b), group["spread"], place["g"].at[b], scale)
        group["spread"].arrived(place["g"].at[b])
        w, up = place["w"], group["up"]
        if colour == 0:
            for half in range(2):
                w[b, 2 * z + half] = joined(place["g"], b, 4 * half, 4)
        else:
            first, second = (y, xpos) if colour == 1 else (xpos, y)
            for half in range(2):
                w[b, first, 2 * second + half] = joined(place["g"], b, 2 * half, 2)
            yield from up[0].gather(middle[colour](b))
        yield from up[-1].gather(place["view"](w, b))
        attend(layer, b, colour)
        trade(layer, b, colour, core).start()
        done()

    def all_sent(b):
        for colour in range(3):
            place, group = places[colour], groups[b][colour]
            group["owners"].scatter_sent(place["last"].at[b])
            group["spread"].gather_sent(place["g"].at[b])
            group["up"][-1].gather_sent(place["view"](place["w"], b))
            if colour:
                group["up"][0].gather_sent(middle[colour](b))

    def finish(layer, b):
        def body(s, carry):
            heads = att[layer, s, :, :, block(b)].reshape(D, BLOCK)
            update = jnp.dot(wo_t[layer], heads, preferred_element_type=f32)
            summed = x[s, :, block(b)].astype(f32) + update
            mean_sq = jnp.mean(summed * summed, axis=0, keepdims=True)
            gains = gain_t[layer]
            normed = summed * lax.rsqrt(mean_sq + EPSILON) * jnp.concatenate([gains, gains], axis=1)
            x[s, :, block(b)] = normed.astype(bf16)
            if layer + 1 == LAYERS:
                far_out(b, s).start()
            return carry

        lax.fori_loop(0, 2, body, 0)
        clock.spend(1.5)

    def far_out(b, s):
        return remote(
            x.at[s, quarter(far_quarter), block(b)], out.at[near_pair + s, :, block(b)],
            o_send.at[b, s], o_recv.at[b, s], partner,
        )

    def own_out(b):
        return pltpu.make_async_copy(
            x.at[:, quarter(own_quarter), block(b)], out.at[pl.ds(near_pair, 2), :, block(b)], o_local.at[b]
        )

    def finish_steps(layer, b):
        yield clock.now + (8.0 if b == 0 else 1.6)
        for colour in range(3):
            trade(layer, b, colour, 1 - core).wait_recv()
        finish(layer, b)
        if layer + 1 < LAYERS:
            project(layer + 1, 0, b)
            project(layer + 1, 1, b)
        else:
            own_out(b).start()

    for layer in range(LAYERS):
        running, order = [], [0]

        def add(steps, running=running, order=order):
            due = next(steps, None)
            if due is not None:
                order[0] += 1
                running.append((due, order[0], steps))

        def launch(b, colour, layer=layer, add=add):
            left[b][colour] = 1

            def done():
                left[b][colour] = 0
                if sum(left[b].values()) == 0 and len(left[b]) == 3:
                    add(finish_steps(layer, b))

            add(colour_steps(layer, b, colour, done))

        left = [{}, {}]
        for colour in range(3):
            launch(0, colour)
        for colour in range(3):
            launch(1, colour)
        for b in range(2):
            project(layer, 2, b)
        fillers = []
        if layer == 0:
            tokens_sent()
            fillers = [functools.partial(turn_out, 0)]
            fillers += [functools.partial(turn_columns, 1, t) for t in range(3)]
            fillers += [functools.partial(turn_out, 1)]
        while running:
            running.sort(key=lambda entry: entry[:2])
            if fillers and running[0][0] > clock.now + 0.7:
                fillers.pop(0)()
                clock.spend(1.0)
                continue
            due, _, steps = running.pop(0)
            clock.now = max(clock.now, due)
            add(steps)
        for filler in fillers:
            filler()
        for b in range(2):
            all_sent(b)
            for colour in range(3):
                trade(layer, b, colour, core).wait_send()

    for b in range(2):
        own_out(b).wait()
        for s in range(2):
            far_out(b, s).wait_send()
            landed = out.at[far_pair + s, :, block(b)]
            remote(landed, landed, o_send.at[b, s], o_recv.at[b, s], partner).wait_recv()


def on_device(tokens, qkv_weight, out_weight, norm_gain):
    scale = 1.0 / (HEAD_DIM * 2 * NX * NY * NZ) ** 0.5
    any_space = pl.BlockSpec(memory_space=pl.ANY)
    vmem = pl.BlockSpec(memory_space=pltpu.VMEM)
    dma = pltpu.SemaphoreType.DMA
    around = lambda n: 2 * (n - 1)
    ring_count = 4 * (around(NZ) + 2 * around(NX) + 2 * around(NY)) + 2 * (around(NZ) + around(NX) + around(NY))
    direct_count = 4 * (NX * NY - 1 + 2 * (NZ - 1))
    result = pl.pallas_call(
        functools.partial(whole, scale),
        out_shape=jax.ShapeDtypeStruct((4, QUARTER, RES), bf16),
        in_specs=[any_space, any_space, any_space, vmem],
        out_specs=any_space,
        scratch_shapes=[
            pltpu.VMEM((2, D, RES), bf16),
            pltpu.VMEM((LAYERS, 3, D, CORE_COLS), bf16),
            pltpu.VMEM((LAYERS, D, D), bf16),
            pltpu.VMEM((LAYERS, 3, CORE_COLS, D), bf16),
            pltpu.VMEM((LAYERS, D, D), bf16),
            pltpu.VMEM((LAYERS, D, 128), f32),
            pltpu.VMEM((LAYERS, 3, CORE_HEADS, 2 * HEAD_DIM, RES), bf16),
            pltpu.VMEM((LAYERS, 2, 2, CORE_COLS, RES), bf16),
            pltpu.VMEM((2, 16, 32, RES), f32),
            pltpu.VMEM((2, 4, 8, 16, RES), f32),
            pltpu.VMEM((2, 4, 8, 16, RES), f32),
            pltpu.VMEM((2, 14, 32, RES), bf16),
            pltpu.VMEM((2, 6, 64, RES), bf16),
            pltpu.VMEM((2, 6, 64, RES), bf16),
            pltpu.VMEM((2, 8, 8, RES), f32),
            pltpu.VMEM((2, 8, 16, RES), f32),
            pltpu.VMEM((2, 8, 16, RES), f32),
            pltpu.VMEM((2, 6, 16, RES), f32),
            pltpu.VMEM((2, 6, 16, RES), f32),
            pltpu.VMEM((2, 4, 8, RES), f32),
            pltpu.VMEM((2, 4, 8, RES), f32),
            pltpu.VMEM((2, 15, 8, RES), f32),
            pltpu.VMEM((2, 7, 8, RES), f32),
            pltpu.VMEM((2, 7, 8, RES), f32),
            pltpu.VMEM((2, 16, 32, RES), bf16),
            pltpu.VMEM((2, 4, 8, 16, RES), bf16),
            pltpu.VMEM((2, 4, 8, 16, RES), bf16),
            pltpu.VMEM((2, 8, 8, RES), bf16),
            pltpu.VMEM((2, 4, 8, RES), bf16),
            pltpu.VMEM((2, 4, 8, RES), bf16),
            pltpu.VMEM((2, 4, 32, RES), bf16),
            pltpu.VMEM((2, 4, 64, RES), bf16),
            pltpu.VMEM((2, 4, 64, RES), bf16),
            pltpu.VMEM((2, 4, 8, 128), f32),
            pltpu.VMEM((2, 4, 8, 128), f32),
            pltpu.VMEM((2, 4, 8, 128), f32),
            pltpu.VMEM((2, 14, 8, 128), f32),
            pltpu.VMEM((2, 6, 8, 128), f32),
            pltpu.VMEM((2, 6, 8, 128), f32),
            dma((2, ring_count)),
            dma((2, direct_count)),
            dma((4 * LAYERS,)),
            dma,
            dma((4,)),
            dma((4,)),
            dma((5,)),
            dma((5,)),
            dma((2, 3)),
            dma((LAYERS, 2, 3)),
            dma((2,)),
            dma((2, 2)),
            dma((2, 2)),
        ],
        compiler_params=pltpu.CompilerParams(
            collective_id=0, has_side_effects=True, vmem_limit_bytes=60 * 1024 * 1024
        ),
    )(
        tokens.transpose(0, 2, 1),
        qkv_weight.transpose(0, 2, 1, 3),
        out_weight,
        norm_gain,
    )
    return result.transpose(0, 2, 1)


def solution(mesh):
    finer = Mesh(mesh.devices.reshape(NY, NX // 2, NZ, 2, 2), AXES)
    rows, heads = ("y", "xh", "z"), ("xl", "core")
    return jax.shard_map(
        on_device,
        mesh=finer,
        in_specs=(P(rows, None, heads), P(), P(), P()),
        out_specs=P(rows, None, heads),
        check_vma=False,
    )
```

```python
import functools

import jax
import jax.numpy as jnp
from jax import lax
from jax.experimental import pallas as pl
from jax.experimental.pallas import tpu as pltpu
from jax.sharding import Mesh
from jax.sharding import PartitionSpec as P

D = 768
HEADS = 12
HEAD_DIM = 64
LAYERS = 2
EPSILON = 1e-06
MESH = pl.DeviceIdType.MESH
AXES = ("y", "xh", "z", "xl", "core")
NX, NY, NZ = 4, 4, 8
RES = 512
BLOCK = RES // 2
CORE_HEADS = HEADS // 2
CORE_COLS = CORE_HEADS * HEAD_DIM
QUARTER = D // 4
f32, bf16 = jnp.float32, jnp.bfloat16

RIGHT, LEFT = 0, 1
LONG, SHORT = 0, 1


def wrap(value, n):
    return lax.rem(value + 2 * n, n)


def remote(src, dst, send_sem, recv_sem, device):
    return pltpu.make_async_remote_copy(
        src_ref=src, dst_ref=dst, send_sem=send_sem, recv_sem=recv_sem, device_id=device, device_id_type=MESH
    )


STEPS = 195.0
LOWEST = 100.0


def encode(value):
    rows, columns = value.shape
    size = jnp.abs(value)
    top = functools.reduce(
        jnp.maximum,
        [size[r : r + 8, c : c + 128] for r in range(0, rows, 8) for c in range(0, columns, 128)],
    )
    top = jnp.maximum(top, 1e-30)
    per_unit = jnp.concatenate([STEPS / top] * (columns // 128), axis=1)
    per_unit = jnp.concatenate([per_unit] * (rows // 8), axis=0)
    level = size * per_unit
    binade = jnp.floor(level)
    code = (1.0 + (level - binade)) * jnp.exp2(binade - LOWEST)
    return jnp.where(value < 0, -code, code).astype(bf16), top / STEPS


def decode(code, unit):
    rows, columns = code.shape
    code = code.astype(f32)
    size = jnp.abs(code)
    binade = jnp.floor(jnp.log2(size))
    level = binade + size * jnp.exp2(-binade) + (LOWEST - 1.0)
    unit = jnp.concatenate([unit] * (columns // 128), axis=1)
    unit = jnp.concatenate([unit] * (rows // 8), axis=0)
    return jnp.where(code < 0, -level, level) * unit


class Clock:
    RATE, FIRST_HOP, NEXT_HOP = 46e3, 3.0, 0.65

    def __init__(self):
        self.now, self.free = 0.0, {}

    def spend(self, time):
        self.now += time

    def send(self, link, size, hops=1):
        begin = max(self.now, self.free.get(link, 0.0))
        self.free[link] = begin + size / self.RATE
        return self.free[link] + self.FIRST_HOP + self.NEXT_HOP * (hops - 1)


class Ring:
    def __init__(self, clock, axis, size, n, pos, right, left, send_sems, recv_sems):
        self.clock, self.axis, self.size = clock, axis, size
        self.n, self.pos, self.devices = n, pos, (right, left)
        self.send_sems, self.recv_sems = send_sems, recv_sems
        self.due = {}

    def hops(self, kind):
        return self.n // 2 - kind

    def half(self, direction, kind):
        return direction ^ kind

    def index(self, direction, kind, hop):
        return direction * (self.n - 1) + kind * (self.n // 2) + hop - 1

    def owner(self, direction, distance):
        return wrap(self.pos + (distance if direction == RIGHT else -distance), self.n)

    def copy(self, src, dst, direction, i):
        return remote(src, dst, self.send_sems(i), self.recv_sems(i), self.devices[direction])

    def start(self, src, dst, direction, kind, hop):
        self.copy(src, dst, direction, self.index(direction, kind, hop)).start()
        self.due[kind, hop] = self.clock.send((self.axis, direction), self.size)

    def each(self):
        for kind in (LONG, SHORT):
            for direction in (RIGHT, LEFT):
                yield direction, kind

    def events(self):
        for hop in range(1, self.n // 2 + 1):
            for kind in (LONG, SHORT):
                if hop <= self.hops(kind):
                    yield kind, hop

    def scatter(self, view, slot):
        for direction, kind in self.each():
            own = view(self.owner(direction, self.hops(kind)), self.half(direction, kind))
            self.start(own, slot(self.index(direction, kind, 1)), direction, kind, 1)
        for kind, hop in self.events():
            yield self.due[kind, hop]
            for direction in (RIGHT, LEFT):
                i = self.index(direction, kind, hop)
                self.copy(slot(i), slot(i), direction, i).wait_recv()
                if hop < self.hops(kind):
                    own = view(self.owner(direction, self.hops(kind) - hop), self.half(direction, kind))
                    slot(i)[...] = slot(i)[...] + own[...]
                    self.start(slot(i), slot(i + 1), direction, kind, hop + 1)
            self.clock.spend(self.size / 500e3)

    def scatter_result(self, view, slot, half):
        total = view(self.pos, half)[...]
        for direction, kind in self.each():
            if self.half(direction, kind) == half:
                total = total + slot(self.index(direction, kind, self.hops(kind)))[...]
        return total

    def scatter_sent(self, slot):
        for direction, kind in self.each():
            for hop in range(1, self.hops(kind) + 1):
                i = self.index(direction, kind, hop)
                self.copy(slot(i), slot(i), direction, i).wait_send()

    def gather(self, view):
        for direction, kind in self.each():
            block = view(self.pos, self.half(direction, kind))
            self.start(block, block, direction, kind, 1)
        for kind, hop in self.events():
            yield self.due[kind, hop]
            for direction in (RIGHT, LEFT):
                i = self.index(direction, kind, hop)
                block = view(self.owner(direction, -hop), self.half(direction, kind))
                self.copy(block, block, direction, i).wait_recv()
                if hop < self.hops(kind):
                    self.start(block, block, direction, kind, hop + 1)

    def gather_sent(self, view):
        for direction, kind in self.each():
            block = view(self.pos, self.half(direction, kind))
            for hop in range(1, self.hops(kind) + 1):
                i = self.index(direction, kind, hop)
                self.copy(block, block, direction, i).wait_send()


class CodedRing(Ring):
    def pair(self, src, dst, direction, i):
        count = 2 * (self.n - 1)
        return self.copy(src[0], dst[0], direction, i), self.copy(src[1], dst[1], direction, count + i)

    def start_pair(self, src, dst, direction, kind, hop):
        for copy in self.pair(src, dst, direction, self.index(direction, kind, hop)):
            copy.start()
        self.due[kind, hop] = self.clock.send((self.axis, direction), self.size + 4096)

    @staticmethod
    def put(place, value):
        codes, units = encode(value)
        place[0][...] = codes
        place[1][...] = units

    @staticmethod
    def get(place):
        return decode(place[0][...], place[1][...])

    def scatter(self, view, slot, staged):
        for direction, kind in self.each():
            place = staged(direction * 2 + kind)
            self.put(place, view(self.owner(direction, self.hops(kind)), self.half(direction, kind)))
            self.start_pair(place, slot(self.index(direction, kind, 1)), direction, kind, 1)
            self.clock.spend(0.1)
        for kind, hop in self.events():
            yield self.due[kind, hop]
            for direction in (RIGHT, LEFT):
                i = self.index(direction, kind, hop)
                for copy in self.pair(slot(i), slot(i), direction, i):
                    copy.wait_recv()
                if hop < self.hops(kind):
                    own = view(self.owner(direction, self.hops(kind) - hop), self.half(direction, kind))
                    self.put(slot(i), self.get(slot(i)) + own)
                    self.start_pair(slot(i), slot(i + 1), direction, kind, hop + 1)
            self.clock.spend(0.4)

    def scatter_result(self, view, slot, half):
        total = view(self.pos, half)
        for direction, kind in self.each():
            if self.half(direction, kind) == half:
                total = total + self.get(slot(self.index(direction, kind, self.hops(kind))))
        return total

    def scatter_sent(self, slot):
        for direction, kind in self.each():
            for hop in range(1, self.hops(kind) + 1):
                i = self.index(direction, kind, hop)
                for copy in self.pair(slot(i), slot(i), direction, i):
                    copy.wait_send()


class Direct:
    def __init__(self, clock, size, peers, pos, owns, send_sems, recv_sems):
        self.clock, self.size, self.peers, self.pos, self.owns = clock, size, peers, pos, owns
        self.send_sems, self.recv_sems = send_sems, recv_sems

    def copy(self, src, dst, k):
        return remote(src, dst, self.send_sems(k), self.recv_sems(k), self.peers[k][0])

    def to_owners(self, action):
        same = [k for k, peer in enumerate(self.peers) if peer[2]]
        other = [k for k, peer in enumerate(self.peers) if not peer[2]]

        @pl.when(self.owns)
        def _():
            for k in same:
                action(k)

        @pl.when(jnp.logical_not(self.owns))
        def _():
            for k in other:
                action(k)

    def price(self, count):
        return max(
            self.clock.send(link, self.size * count / len(self.peers), hops) for _, _, _, link, hops in self.peers
        )

    def scatter_start(self, blocks, slots):
        self.to_owners(lambda k: self.copy(blocks.at[self.peers[k][1]], slots(k), k).start())
        return self.price(len(self.peers) // 2)

    def turn(self, blocks, slots, spread, weights, scale):
        every = range(len(self.peers))

        @pl.when(self.owns)
        def _():
            for k in every:
                self.copy(slots(k), slots(k), k).wait_recv()
            total = blocks[self.pos]
            for k in every:
                total = total + slots(k)[...]
            weights[self.pos] = softmax(total, scale)
            for k in every:
                spread.copy(weights.at[self.pos], weights.at[self.pos], k).start()

        self.clock.spend(0.6)
        return spread.price(len(self.peers) // 2)

    def arrived(self, blocks):
        self.to_owners(lambda k: self.copy(blocks.at[self.pos], blocks.at[self.pos], k).wait_recv())

    def scatter_sent(self, blocks):
        self.to_owners(lambda k: self.copy(blocks.at[self.pos], blocks.at[self.pos], k).wait_send())

    def gather_sent(self, blocks):
        @pl.when(self.owns)
        def _():
            for k in range(len(self.peers)):
                self.copy(blocks.at[self.pos], blocks.at[self.pos], k).wait_send()


def softmax(scores, scale):
    shifted = (scores - jnp.max(scores, axis=-1, keepdims=True)) * scale
    grown = jnp.exp(shifted)
    return (grown / jnp.sum(grown, axis=-1, keepdims=True)).astype(bf16)


def whole(
    scale, tok, wqkv, wo, gain, out,
    x, wq_in, wo_in, wq_t, wo_t, gain_t, qkv, att,
    s_a, s_b, s_c, r_a, r_b, r_c, acc_a, acc_b, acc_c, r_b2, r_c2, acc_b2, acc_c2, d_a, d_b, d_c,
    w_a, w_b, w_c, g_a, g_b, g_c, e_a, e_b, e_c, ue_a, ue_b, ue_c, ur_a, ur_b, ur_c, ring_sems, direct_sems,
    w_sems, x_local, x_send, x_recv, f_send, f_recv, t_send, t_recv, o_local, o_send, o_recv,
):
    y, xh, z = lax.axis_index("y"), lax.axis_index("xh"), lax.axis_index("z")
    xl, core = lax.axis_index("xl"), lax.axis_index("core")
    xpos = xh * 2 + xl

    def at_x(p):
        return {"xh": lax.div(p, 2), "xl": lax.rem(p, 2)}

    x_right, x_left = at_x(wrap(xpos + 1, NX)), at_x(wrap(xpos - 1, NX))
    y_right, y_left = {"y": wrap(y + 1, NY)}, {"y": wrap(y - 1, NY)}
    z_right, z_left = {"z": wrap(z + 1, NZ)}, {"z": wrap(z - 1, NZ)}
    plane = []
    for dx in range(NX):
        for dy in range(NY):
            if dx or dy:
                px, py = wrap(xpos + dx, NX), wrap(y + dy, NY)
                link = ("x", int(dx > NX // 2)) if dx else ("y", int(dy > NY // 2))
                far = min(dx, NX - dx) + min(dy, NY - dy)
                index = px * (NY // 2) + lax.div(py, 2)
                plane.append(({**at_x(px), "y": py}, index, (dx + dy) % 2 == 0, link, far))
    along_z = []
    for dz in range(1, NZ):
        pz = wrap(z + dz, NZ)
        along_z.append(({"z": pz}, lax.div(pz, 2), dz % 2 == 0, ("z", int(dz > NZ // 2)), min(dz, NZ - dz)))
    other_core = {"core": 1 - core}
    partner = {"xl": 1 - xl}

    loads = []
    for layer in range(LAYERS):
        for t in range(3):
            loads.append(
                pltpu.make_async_copy(
                    wqkv.at[layer, t, :, pl.ds(pl.multiple_of(core * CORE_COLS, 128), CORE_COLS)],
                    wq_in.at[layer, t],
                    w_sems.at[layer * 4 + t],
                )
            )
        loads.append(pltpu.make_async_copy(wo.at[layer], wo_in.at[layer], w_sems.at[layer * 4 + 3]))
    own_quarter, far_quarter = 2 * xl + core, 2 * (1 - xl) + core
    near_pair, far_pair = 2 * xl, 2 * (1 - xl)

    def quarter(q):
        return pl.ds(pl.multiple_of(q * QUARTER, 64), QUARTER)

    own_tokens = pltpu.make_async_copy(tok.at[pl.ds(near_pair, 2)], x.at[:, quarter(own_quarter)], x_local)
    own_tokens.start()
    for load in loads:
        load.start()

    barrier = pltpu.get_barrier_semaphore()
    partners = [peer[0] for peer in plane + along_z] + [other_core]
    for device in partners:
        pl.semaphore_signal(barrier, inc=1, device_id=device, device_id_type=MESH)
    pl.semaphore_wait(barrier, len(partners))

    def block(b):
        return slice(b * BLOCK, (b + 1) * BLOCK)

    pieces = [(b, s) for b in range(2) for s in range(2)]

    def piece(q, b, s):
        return x.at[s, quarter(q), block(b)]

    for k, (b, s) in enumerate(pieces):
        remote(
            tok.at[far_pair + s, :, block(b)], piece(own_quarter, b, s), x_send.at[k], x_recv.at[k], partner
        ).start()
    remote(
        tok.at[pl.ds(near_pair, 2)], x.at[:, quarter(own_quarter)], f_send.at[4], f_recv.at[4], other_core
    ).start()

    def turn_columns(layer, t):
        loads[layer * 4 + t].wait()
        wq_t[layer, t] = wq_in[layer, t].T

    def turn_out(layer):
        loads[layer * 4 + 3].wait()
        for m in range(3):
            wo_t[layer, m * 256 : (m + 1) * 256] = wo_in[layer, :, m * 256 : (m + 1) * 256].T
        row = gain[layer : layer + 1, :].astype(f32)
        gain_t[layer] = jnp.broadcast_to(row, (128, D)).T

    clock = Clock()

    def project(layer, t, b):
        for s in range(2):
            columns = jnp.dot(wq_t[layer, t], x[s, :, block(b)], preferred_element_type=f32)
            qkv[layer, t, :, s * HEAD_DIM : (s + 1) * HEAD_DIM, block(b)] = columns.astype(bf16).reshape(
                CORE_HEADS, HEAD_DIM, BLOCK
            )
        clock.spend(0.5)

    turn_columns(0, 0)
    turn_columns(0, 1)
    for k, (b, s) in enumerate(pieces):
        arrived = piece(far_quarter, b, s)
        remote(arrived, arrived, x_send.at[k], x_recv.at[k], partner).wait_recv()
        remote(arrived, arrived, f_send.at[k], f_recv.at[k], other_core).start()
        if k == 0:
            turn_columns(0, 2)
            own_tokens.wait()
            near = x.at[:, quarter(2 * xl + 1 - core)]
            remote(near, near, f_send.at[4], f_recv.at[4], other_core).wait_recv()
        if k == 2:
            for j in range(2):
                arrived = piece(2 * (1 - xl) + 1 - core, *pieces[j])
                remote(arrived, arrived, f_send.at[j], f_recv.at[j], other_core).wait_recv()
            project(0, 0, 0)
            project(0, 1, 0)
    for j in range(2, 4):
        arrived = piece(2 * (1 - xl) + 1 - core, *pieces[j])
        remote(arrived, arrived, f_send.at[j], f_recv.at[j], other_core).wait_recv()
    project(0, 0, 1)
    project(0, 1, 1)

    def tokens_sent():
        for k, (b, s) in enumerate(pieces):
            arrived = piece(far_quarter, b, s)
            remote(arrived, arrived, x_send.at[k], x_recv.at[k], partner).wait_send()
            remote(arrived, arrived, f_send.at[k], f_recv.at[k], other_core).wait_send()
        near = x.at[:, quarter(own_quarter)]
        remote(near, near, f_send.at[4], f_recv.at[4], other_core).wait_send()

    plane_pos = xpos * (NY // 2) + lax.div(y, 2)
    z_pos = lax.div(z, 2)
    plane_parity, z_parity = lax.rem(xpos + y, 2), lax.rem(z, 2)

    def taker(table):
        taken = [0]

        def take(count):
            first = taken[0]
            taken[0] += count
            return lambda i: table.at[first + i]

        return take

    row = RES * 4

    def colour_rings(b):
        take_ring, take_direct = taker(ring_sems.at[b]), taker(direct_sems.at[b])

        def ring(axis, rows, width, kind=Ring):
            n, pos, right, left = {
                "x": (NX, xpos, x_right, x_left),
                "y": (NY, y, y_right, y_left),
                "z": (NZ, z, z_right, z_left),
            }[axis]
            count = 2 * (n - 1) * (2 if kind is CodedRing else 1)
            return kind(clock, axis, rows * row * width, n, pos, right, left, take_ring(count), take_ring(count))

        def direct(peers, width):
            pos, parity = (plane_pos, plane_parity) if peers is plane else (z_pos, z_parity)
            return Direct(
                clock, 8 * row * width, peers, pos, parity == b, take_direct(len(peers)), take_direct(len(peers))
            )

        return [
            dict(
                down=[ring("z", 32, 0.5, CodedRing)], owners=direct(plane, 1), spread=direct(plane, 0.5), up=[ring("z", 32, 0.5)]
            )
        ] + [
            dict(
                down=[ring(first, 64, 0.5, CodedRing), ring(second, 16, 1)],
                owners=direct(along_z, 1),
                spread=direct(along_z, 0.5),
                up=[ring(second, 16, 0.5), ring(first, 64, 0.5)],
            )
            for first, second in (("y", "x"), ("x", "y"))
        ]

    groups = [colour_rings(b) for b in range(2)]

    def slots(ref, b):
        return lambda i: ref.at[b, i]

    def pairs(ref, b):
        return lambda owner, half: ref.at[b, 2 * owner + half]

    def fours(ref, b):
        return lambda owner, half: ref.at[b, owner, pl.ds(4 * half, 4)]

    def coded(codes, units, b):
        return lambda i: (codes.at[b, i], units.at[b, i])

    def terms(view):
        return lambda owner, half: view(owner, half)[...].reshape(-1, RES)

    places = [
        dict(s=s_a, r=(r_a, ur_a), e=(e_a, ue_a), r2=None, acc=None, last=acc_a, d=d_a, w=w_a, g=g_a, view=pairs, blocks=(8, 32)),
        dict(s=s_b, r=(r_b, ur_b), e=(e_b, ue_b), r2=r_b2, acc=acc_b, last=acc_b2, d=d_b, w=w_b, g=g_b, view=fours, blocks=(2, 8, 16)),
        dict(s=s_c, r=(r_c, ur_c), e=(e_c, ue_c), r2=r_c2, acc=acc_c, last=acc_c2, d=d_c, w=w_c, g=g_c, view=fours, blocks=(2, 8, 16)),
    ]
    middle = [None, lambda b: lambda owner, half: w_b.at[b, y, 2 * owner + half],
              lambda b: lambda owner, half: w_c.at[b, xpos, 2 * owner + half]]

    def trade(layer, b, colour, owner):
        part = att.at[layer, :, owner, pl.ds(128 * colour, 128), block(b)]
        return remote(part, part, t_send.at[b, colour], t_recv.at[layer, b, colour], other_core)

    def score(layer, b, colour):
        place = places[colour]
        blocks = place["blocks"]

        def body(h, carry):
            head = 2 * colour + h
            scores = jnp.dot(
                qkv[layer, 0, head, :, block(b)].T, qkv[layer, 1, head], preferred_element_type=f32
            )
            place["s"][b, pl.ds(h * blocks[0], blocks[0])] = scores.reshape(*blocks, RES)
            return carry

        lax.fori_loop(0, 2, body, 0)
        clock.spend(0.5)

    def attend(layer, b, colour):
        place = places[colour]
        blocks = place["blocks"]

        def body(h, carry):
            head = 2 * colour + h
            weights = place["w"][b, pl.ds(h * blocks[0], blocks[0])].reshape(BLOCK, RES)
            heads = lax.dot_general(
                qkv[layer, 2, head], weights, (((1,), (1,)), ((), ())), preferred_element_type=f32
            ).astype(bf16)
            at = pl.ds(pl.multiple_of(head * HEAD_DIM, HEAD_DIM), HEAD_DIM)
            for s in range(2):
                att[layer, s, core, at, block(b)] = heads[s * HEAD_DIM : (s + 1) * HEAD_DIM]
            return carry

        lax.fori_loop(0, 2, body, 0)
        clock.spend(0.6)

    def joined(ref, b, first, blocks):
        return ref[b, first : first + blocks].astype(f32).reshape(blocks * 8, RES).astype(bf16)

    def colour_steps(layer, b, colour, done):
        place, group = places[colour], groups[b][colour]
        view, slot, staged = terms(place["view"](place["s"], b)), coded(*place["r"], b), coded(*place["e"], b)
        score(layer, b, colour)
        down = group["down"]
        yield from down[0].scatter(view, slot, staged)
        last = place["last"].at[b]
        if colour == 0:
            for half in range(2):
                last[4 * half : 4 * half + 4] = down[0].scatter_result(view, slot, half).reshape(4, 8, RES)
        else:
            view2, slot2 = pairs(place["acc"], b), slots(place["r2"], b)
            for half in range(2):
                place["acc"][b, 4 * half : 4 * half + 4] = down[0].scatter_result(view, slot, half).reshape(4, 16, RES)
            yield from down[1].scatter(view2, slot2)
            for half in range(2):
                last[2 * half : 2 * half + 2] = down[1].scatter_result(view2, slot2, half).reshape(2, 8, RES)
            down[1].scatter_sent(slot2)
        down[0].scatter_sent(slot)
        yield group["owners"].scatter_start(last, slots(place["d"], b))
        yield group["owners"].turn(last, slots(place["d"], b), group["spread"], place["g"].at[b], scale)
        group["spread"].arrived(place["g"].at[b])
        w, up = place["w"], group["up"]
        if colour == 0:
            for half in range(2):
                w[b, 2 * z + half] = joined(place["g"], b, 4 * half, 4)
        else:
            first, second = (y, xpos) if colour == 1 else (xpos, y)
            for half in range(2):
                w[b, first, 2 * second + half] = joined(place["g"], b, 2 * half, 2)
            yield from up[0].gather(middle[colour](b))
        yield from up[-1].gather(place["view"](w, b))
        attend(layer, b, colour)
        trade(layer, b, colour, core).start()
        done()

    def all_sent(b):
        for colour in range(3):
            place, group = places[colour], groups[b][colour]
            group["owners"].scatter_sent(place["last"].at[b])
            group["spread"].gather_sent(place["g"].at[b])
            group["up"][-1].gather_sent(place["view"](place["w"], b))
            if colour:
                group["up"][0].gather_sent(middle[colour](b))

    def finish(layer, b):
        def body(s, carry):
            heads = att[layer, s, :, :, block(b)].reshape(D, BLOCK)
            update = jnp.dot(wo_t[layer], heads, preferred_element_type=f32)
            summed = x[s, :, block(b)].astype(f32) + update
            mean_sq = jnp.mean(summed * summed, axis=0, keepdims=True)
            gains = gain_t[layer]
            normed = summed * lax.rsqrt(mean_sq + EPSILON) * jnp.concatenate([gains, gains], axis=1)
            x[s, :, block(b)] = normed.astype(bf16)
            if layer + 1 == LAYERS:
                far_out(b, s).start()
            return carry

        lax.fori_loop(0, 2, body, 0)
        clock.spend(1.5)

    def far_out(b, s):
        return remote(
            x.at[s, quarter(far_quarter), block(b)], out.at[near_pair + s, :, block(b)],
            o_send.at[b, s], o_recv.at[b, s], partner,
        )

    def own_out(b):
        return pltpu.make_async_copy(
            x.at[:, quarter(own_quarter), block(b)], out.at[pl.ds(near_pair, 2), :, block(b)], o_local.at[b]
        )

    def finish_steps(layer, b):
        yield clock.now + ((2.4, 2.4)[layer] if b == 0 else 1.6)
        for colour in range(3):
            trade(layer, b, colour, 1 - core).wait_recv()
        finish(layer, b)
        if layer + 1 < LAYERS:
            project(layer + 1, 0, b)
            project(layer + 1, 1, b)
        else:
            own_out(b).start()

    for layer in range(LAYERS):
        running, order = [], [0]

        def add(steps, running=running, order=order):
            due = next(steps, None)
            if due is not None:
                order[0] += 1
                running.append((due, order[0], steps))

        def launch(b, colour, layer=layer, add=add):
            left[b][colour] = 1

            def done():
                left[b][colour] = 0
                if sum(left[b].values()) == 0 and len(left[b]) == 3:
                    add(finish_steps(layer, b))

            add(colour_steps(layer, b, colour, done))

        left = [{}, {}]
        for colour in range(3):
            launch(0, colour)
        for colour in range(3):
            launch(1, colour)
        for b in range(2):
            project(layer, 2, b)
        fillers = []
        if layer == 0:
            tokens_sent()
            fillers = [functools.partial(turn_out, 0)]
            fillers += [functools.partial(turn_columns, 1, t) for t in range(3)]
            fillers += [functools.partial(turn_out, 1)]
        while running:
            running.sort(key=lambda entry: entry[:2])
            if fillers and running[0][0] > clock.now + 0.7:
                fillers.pop(0)()
                clock.spend(1.0)
                continue
            due, _, steps = running.pop(0)
            clock.now = max(clock.now, due)
            add(steps)
        for filler in fillers:
            filler()
        for b in range(2):
            all_sent(b)
            for colour in range(3):
                trade(layer, b, colour, core).wait_send()

    for b in range(2):
        own_out(b).wait()
        for s in range(2):
            far_out(b, s).wait_send()
            landed = out.at[far_pair + s, :, block(b)]
            remote(landed, landed, o_send.at[b, s], o_recv.at[b, s], partner).wait_recv()


def on_device(tokens, qkv_weight, out_weight, norm_gain):
    scale = 1.0 / (HEAD_DIM * 2 * NX * NY * NZ) ** 0.5
    any_space = pl.BlockSpec(memory_space=pl.ANY)
    vmem = pl.BlockSpec(memory_space=pltpu.VMEM)
    dma = pltpu.SemaphoreType.DMA
    around = lambda n: 2 * (n - 1)
    ring_count = 4 * (around(NZ) + 2 * around(NX) + 2 * around(NY)) + 2 * (around(NZ) + around(NX) + around(NY))
    direct_count = 4 * (NX * NY - 1 + 2 * (NZ - 1))
    result = pl.pallas_call(
        functools.partial(whole, scale),
        out_shape=jax.ShapeDtypeStruct((4, QUARTER, RES), bf16),
        in_specs=[any_space, any_space, any_space, vmem],
        out_specs=any_space,
        scratch_shapes=[
            pltpu.VMEM((2, D, RES), bf16),
            pltpu.VMEM((LAYERS, 3, D, CORE_COLS), bf16),
            pltpu.VMEM((LAYERS, D, D), bf16),
            pltpu.VMEM((LAYERS, 3, CORE_COLS, D), bf16),
            pltpu.VMEM((LAYERS, D, D), bf16),
            pltpu.VMEM((LAYERS, D, 128), f32),
            pltpu.VMEM((LAYERS, 3, CORE_HEADS, 2 * HEAD_DIM, RES), bf16),
            pltpu.VMEM((LAYERS, 2, 2, CORE_COLS, RES), bf16),
            pltpu.VMEM((2, 16, 32, RES), f32),
            pltpu.VMEM((2, 4, 8, 16, RES), f32),
            pltpu.VMEM((2, 4, 8, 16, RES), f32),
            pltpu.VMEM((2, 14, 32, RES), bf16),
            pltpu.VMEM((2, 6, 64, RES), bf16),
            pltpu.VMEM((2, 6, 64, RES), bf16),
            pltpu.VMEM((2, 8, 8, RES), f32),
            pltpu.VMEM((2, 8, 16, RES), f32),
            pltpu.VMEM((2, 8, 16, RES), f32),
            pltpu.VMEM((2, 6, 16, RES), f32),
            pltpu.VMEM((2, 6, 16, RES), f32),
            pltpu.VMEM((2, 4, 8, RES), f32),
            pltpu.VMEM((2, 4, 8, RES), f32),
            pltpu.VMEM((2, 15, 8, RES), f32),
            pltpu.VMEM((2, 7, 8, RES), f32),
            pltpu.VMEM((2, 7, 8, RES), f32),
            pltpu.VMEM((2, 16, 32, RES), bf16),
            pltpu.VMEM((2, 4, 8, 16, RES), bf16),
            pltpu.VMEM((2, 4, 8, 16, RES), bf16),
            pltpu.VMEM((2, 8, 8, RES), bf16),
            pltpu.VMEM((2, 4, 8, RES), bf16),
            pltpu.VMEM((2, 4, 8, RES), bf16),
            pltpu.VMEM((2, 4, 32, RES), bf16),
            pltpu.VMEM((2, 4, 64, RES), bf16),
            pltpu.VMEM((2, 4, 64, RES), bf16),
            pltpu.VMEM((2, 4, 8, 128), f32),
            pltpu.VMEM((2, 4, 8, 128), f32),
            pltpu.VMEM((2, 4, 8, 128), f32),
            pltpu.VMEM((2, 14, 8, 128), f32),
            pltpu.VMEM((2, 6, 8, 128), f32),
            pltpu.VMEM((2, 6, 8, 128), f32),
            dma((2, ring_count)),
            dma((2, direct_count)),
            dma((4 * LAYERS,)),
            dma,
            dma((4,)),
            dma((4,)),
            dma((5,)),
            dma((5,)),
            dma((2, 3)),
            dma((LAYERS, 2, 3)),
            dma((2,)),
            dma((2, 2)),
            dma((2, 2)),
        ],
        compiler_params=pltpu.CompilerParams(
            collective_id=0, has_side_effects=True, vmem_limit_bytes=60 * 1024 * 1024
        ),
    )(
        tokens.transpose(0, 2, 1),
        qkv_weight.transpose(0, 2, 1, 3),
        out_weight,
        norm_gain,
    )
    return result.transpose(0, 2, 1)


def solution(mesh):
    finer = Mesh(mesh.devices.reshape(NY, NX // 2, NZ, 2, 2), AXES)
    rows, heads = ("y", "xh", "z"), ("xl", "core")
    return jax.shard_map(
        on_device,
        mesh=finer,
        in_specs=(P(rows, None, heads), P(), P(), P()),
        out_specs=P(rows, None, heads),
        check_vma=False,
    )
```

```python
import functools

import jax
import jax.numpy as jnp
from jax import lax
from jax.experimental import pallas as pl
from jax.experimental.pallas import tpu as pltpu
from jax.sharding import Mesh
from jax.sharding import PartitionSpec as P

D = 768
HEADS = 12
HEAD_DIM = 64
LAYERS = 2
EPSILON = 1e-06
MESH = pl.DeviceIdType.MESH
AXES = ("y", "xh", "z", "xl", "core")
NX, NY, NZ = 4, 4, 8
RES = 512
BLOCK = RES // 2
CORE_HEADS = HEADS // 2
CORE_COLS = CORE_HEADS * HEAD_DIM
QUARTER = D // 4
f32, bf16 = jnp.float32, jnp.bfloat16

RIGHT, LEFT = 0, 1
LONG, SHORT = 0, 1


def wrap(value, n):
    return lax.rem(value + 2 * n, n)


def remote(src, dst, send_sem, recv_sem, device):
    return pltpu.make_async_remote_copy(
        src_ref=src, dst_ref=dst, send_sem=send_sem, recv_sem=recv_sem, device_id=device, device_id_type=MESH
    )


STEPS = 195.0
LOWEST = 100.0


def encode(value):
    rows, columns = value.shape
    size = jnp.abs(value)
    top = functools.reduce(
        jnp.maximum,
        [size[r : r + 8, c : c + 128] for r in range(0, rows, 8) for c in range(0, columns, 128)],
    )
    top = jnp.maximum(top, 1e-30)
    per_unit = jnp.concatenate([STEPS / top] * (columns // 128), axis=1)
    per_unit = jnp.concatenate([per_unit] * (rows // 8), axis=0)
    level = size * per_unit
    binade = jnp.floor(level)
    code = (1.0 + (level - binade)) * jnp.exp2(binade - LOWEST)
    return jnp.where(value < 0, -code, code).astype(bf16), top / STEPS


def decode(code, unit):
    rows, columns = code.shape
    code = code.astype(f32)
    size = jnp.abs(code)
    binade = jnp.floor(jnp.log2(size))
    level = binade + size * jnp.exp2(-binade) + (LOWEST - 1.0)
    unit = jnp.concatenate([unit] * (columns // 128), axis=1)
    unit = jnp.concatenate([unit] * (rows // 8), axis=0)
    return jnp.where(code < 0, -level, level) * unit


class Clock:
    RATE, FIRST_HOP, NEXT_HOP = 46e3, 3.0, 0.65

    def __init__(self):
        self.now, self.free = 0.0, {}

    def spend(self, time):
        self.now += time

    def send(self, link, size, hops=1):
        begin = max(self.now, self.free.get(link, 0.0))
        self.free[link] = begin + size / self.RATE
        return self.free[link] + self.FIRST_HOP + self.NEXT_HOP * (hops - 1)


class Ring:
    def __init__(self, clock, axis, size, n, pos, right, left, send_sems, recv_sems):
        self.clock, self.axis, self.size = clock, axis, size
        self.n, self.pos, self.devices = n, pos, (right, left)
        self.send_sems, self.recv_sems = send_sems, recv_sems
        self.due = {}

    def hops(self, kind):
        return self.n // 2 - kind

    def half(self, direction, kind):
        return direction ^ kind

    def index(self, direction, kind, hop):
        return direction * (self.n - 1) + kind * (self.n // 2) + hop - 1

    def owner(self, direction, distance):
        return wrap(self.pos + (distance if direction == RIGHT else -distance), self.n)

    def copy(self, src, dst, direction, i):
        return remote(src, dst, self.send_sems(i), self.recv_sems(i), self.devices[direction])

    def start(self, src, dst, direction, kind, hop):
        self.copy(src, dst, direction, self.index(direction, kind, hop)).start()
        self.due[kind, hop] = self.clock.send((self.axis, direction), self.size)

    def each(self):
        for kind in (LONG, SHORT):
            for direction in (RIGHT, LEFT):
                yield direction, kind

    def events(self):
        for hop in range(1, self.n // 2 + 1):
            for kind in (LONG, SHORT):
                if hop <= self.hops(kind):
                    yield kind, hop

    def scatter(self, view, slot):
        for direction, kind in self.each():
            own = view(self.owner(direction, self.hops(kind)), self.half(direction, kind))
            self.start(own, slot(self.index(direction, kind, 1)), direction, kind, 1)
        for kind, hop in self.events():
            yield self.due[kind, hop]
            for direction in (RIGHT, LEFT):
                i = self.index(direction, kind, hop)
                self.copy(slot(i), slot(i), direction, i).wait_recv()
                if hop < self.hops(kind):
                    own = view(self.owner(direction, self.hops(kind) - hop), self.half(direction, kind))
                    slot(i)[...] = slot(i)[...] + own[...]
                    self.start(slot(i), slot(i + 1), direction, kind, hop + 1)
            self.clock.spend(self.size / 500e3)

    def scatter_result(self, view, slot, half):
        total = view(self.pos, half)[...]
        for direction, kind in self.each():
            if self.half(direction, kind) == half:
                total = total + slot(self.index(direction, kind, self.hops(kind)))[...]
        return total

    def scatter_sent(self, slot):
        for direction, kind in self.each():
            for hop in range(1, self.hops(kind) + 1):
                i = self.index(direction, kind, hop)
                self.copy(slot(i), slot(i), direction, i).wait_send()

    def gather(self, view):
        for direction, kind in self.each():
            block = view(self.pos, self.half(direction, kind))
            self.start(block, block, direction, kind, 1)
        for kind, hop in self.events():
            yield self.due[kind, hop]
            for direction in (RIGHT, LEFT):
                i = self.index(direction, kind, hop)
                block = view(self.owner(direction, -hop), self.half(direction, kind))
                self.copy(block, block, direction, i).wait_recv()
                if hop < self.hops(kind):
                    self.start(block, block, direction, kind, hop + 1)

    def gather_sent(self, view):
        for direction, kind in self.each():
            block = view(self.pos, self.half(direction, kind))
            for hop in range(1, self.hops(kind) + 1):
                i = self.index(direction, kind, hop)
                self.copy(block, block, direction, i).wait_send()


class CodedRing(Ring):
    def pair(self, src, dst, direction, i):
        count = 2 * (self.n - 1)
        return self.copy(src[0], dst[0], direction, i), self.copy(src[1], dst[1], direction, count + i)

    def start_pair(self, src, dst, direction, kind, hop):
        for copy in self.pair(src, dst, direction, self.index(direction, kind, hop)):
            copy.start()
        self.due[kind, hop] = self.clock.send((self.axis, direction), self.size + 4096)

    @staticmethod
    def put(place, value):
        codes, units = encode(value)
        place[0][...] = codes
        place[1][...] = units

    @staticmethod
    def get(place):
        return decode(place[0][...], place[1][...])

    def scatter(self, view, slot, staged):
        for direction, kind in self.each():
            place = staged(direction * 2 + kind)
            self.put(place, view(self.owner(direction, self.hops(kind)), self.half(direction, kind)))
            self.start_pair(place, slot(self.index(direction, kind, 1)), direction, kind, 1)
            self.clock.spend(0.1)
        for kind, hop in self.events():
            yield self.due[kind, hop]
            for direction in (RIGHT, LEFT):
                i = self.index(direction, kind, hop)
                for copy in self.pair(slot(i), slot(i), direction, i):
                    copy.wait_recv()
                if hop < self.hops(kind):
                    own = view(self.owner(direction, self.hops(kind) - hop), self.half(direction, kind))
                    self.put(slot(i), self.get(slot(i)) + own)
                    self.start_pair(slot(i), slot(i + 1), direction, kind, hop + 1)
            self.clock.spend(0.4)

    def scatter_result(self, view, slot, half):
        total = view(self.pos, half)
        for direction, kind in self.each():
            if self.half(direction, kind) == half:
                total = total + self.get(slot(self.index(direction, kind, self.hops(kind))))
        return total

    def scatter_sent(self, slot):
        for direction, kind in self.each():
            for hop in range(1, self.hops(kind) + 1):
                i = self.index(direction, kind, hop)
                for copy in self.pair(slot(i), slot(i), direction, i):
                    copy.wait_send()


class Direct:
    def __init__(self, clock, size, peers, pos, owns, send_sems, recv_sems):
        self.clock, self.size, self.peers, self.pos, self.owns = clock, size, peers, pos, owns
        self.send_sems, self.recv_sems = send_sems, recv_sems

    def copy(self, src, dst, k):
        return remote(src, dst, self.send_sems(k), self.recv_sems(k), self.peers[k][0])

    def to_owners(self, action):
        same = [k for k, peer in enumerate(self.peers) if peer[2]]
        other = [k for k, peer in enumerate(self.peers) if not peer[2]]

        @pl.when(self.owns)
        def _():
            for k in same:
                action(k)

        @pl.when(jnp.logical_not(self.owns))
        def _():
            for k in other:
                action(k)

    def price(self, count):
        return max(
            self.clock.send(link, self.size * count / len(self.peers), hops) for _, _, _, link, hops in self.peers
        )

    def scatter_start(self, blocks, slots):
        self.to_owners(lambda k: self.copy(blocks.at[self.peers[k][1]], slots(k), k).start())
        return self.price(len(self.peers) // 2)

    def turn(self, blocks, slots, spread, weights, scale):
        every = range(len(self.peers))

        @pl.when(self.owns)
        def _():
            for k in every:
                self.copy(slots(k), slots(k), k).wait_recv()
            total = blocks[self.pos]
            for k in every:
                total = total + slots(k)[...]
            weights[self.pos] = softmax(total, scale)
            for k in every:
                spread.copy(weights.at[self.pos], weights.at[self.pos], k).start()

        self.clock.spend(0.6)
        return spread.price(len(self.peers) // 2)

    def arrived(self, blocks):
        self.to_owners(lambda k: self.copy(blocks.at[self.pos], blocks.at[self.pos], k).wait_recv())

    def scatter_sent(self, blocks):
        self.to_owners(lambda k: self.copy(blocks.at[self.pos], blocks.at[self.pos], k).wait_send())

    def gather_sent(self, blocks):
        @pl.when(self.owns)
        def _():
            for k in range(len(self.peers)):
                self.copy(blocks.at[self.pos], blocks.at[self.pos], k).wait_send()


def softmax(scores, scale):
    shifted = (scores - jnp.max(scores, axis=-1, keepdims=True)) * scale
    grown = jnp.exp(shifted)
    return (grown / jnp.sum(grown, axis=-1, keepdims=True)).astype(bf16)


def whole(
    scale, tok, wqkv, wo, gain, out,
    x, wq_in, wo_in, wq_t, wo_t, gain_t, qkv, att,
    s_a, s_b, s_c, r_a, r_b, r_c, acc_a, acc_b, acc_c, r_b2, r_c2, acc_b2, acc_c2, d_a, d_b, d_c,
    w_a, w_b, w_c, g_a, g_b, g_c, e_a, e_b, e_c, ue_a, ue_b, ue_c, ur_a, ur_b, ur_c, ring_sems, direct_sems,
    w_sems, x_local, x_send, x_recv, f_send, f_recv, t_send, t_recv, o_local, o_send, o_recv,
):
    y, xh, z = lax.axis_index("y"), lax.axis_index("xh"), lax.axis_index("z")
    xl, core = lax.axis_index("xl"), lax.axis_index("core")
    xpos = xh * 2 + xl

    def at_x(p):
        return {"xh": lax.div(p, 2), "xl": lax.rem(p, 2)}

    x_right, x_left = at_x(wrap(xpos + 1, NX)), at_x(wrap(xpos - 1, NX))
    y_right, y_left = {"y": wrap(y + 1, NY)}, {"y": wrap(y - 1, NY)}
    z_right, z_left = {"z": wrap(z + 1, NZ)}, {"z": wrap(z - 1, NZ)}
    plane = []
    for dx in range(NX):
        for dy in range(NY):
            if dx or dy:
                px, py = wrap(xpos + dx, NX), wrap(y + dy, NY)
                link = ("x", int(dx > NX // 2)) if dx else ("y", int(dy > NY // 2))
                far = min(dx, NX - dx) + min(dy, NY - dy)
                index = px * (NY // 2) + lax.div(py, 2)
                plane.append(({**at_x(px), "y": py}, index, (dx + dy) % 2 == 0, link, far))
    along_z = []
    for dz in range(1, NZ):
        pz = wrap(z + dz, NZ)
        along_z.append(({"z": pz}, lax.div(pz, 2), dz % 2 == 0, ("z", int(dz > NZ // 2)), min(dz, NZ - dz)))
    other_core = {"core": 1 - core}
    partner = {"xl": 1 - xl}

    loads = []
    for layer in range(LAYERS):
        for t in range(3):
            loads.append(
                pltpu.make_async_copy(
                    wqkv.at[layer, t, :, pl.ds(pl.multiple_of(core * CORE_COLS, 128), CORE_COLS)],
                    wq_in.at[layer, t],
                    w_sems.at[layer * 4 + t],
                )
            )
        loads.append(pltpu.make_async_copy(wo.at[layer], wo_in.at[layer], w_sems.at[layer * 4 + 3]))
    own_quarter, far_quarter = 2 * xl + core, 2 * (1 - xl) + core
    near_pair, far_pair = 2 * xl, 2 * (1 - xl)

    def quarter(q):
        return pl.ds(pl.multiple_of(q * QUARTER, 64), QUARTER)

    own_tokens = pltpu.make_async_copy(tok.at[pl.ds(near_pair, 2)], x.at[:, quarter(own_quarter)], x_local)
    own_tokens.start()
    for load in loads:
        load.start()

    barrier = pltpu.get_barrier_semaphore()
    partners = [peer[0] for peer in plane + along_z] + [other_core]
    for device in partners:
        pl.semaphore_signal(barrier, inc=1, device_id=device, device_id_type=MESH)
    pl.semaphore_wait(barrier, len(partners))

    def block(b):
        return slice(b * BLOCK, (b + 1) * BLOCK)

    pieces = [(b, s) for b in range(2) for s in range(2)]

    def piece(q, b, s):
        return x.at[s, quarter(q), block(b)]

    for k, (b, s) in enumerate(pieces):
        remote(
            tok.at[far_pair + s, :, block(b)], piece(own_quarter, b, s), x_send.at[k], x_recv.at[k], partner
        ).start()
    remote(
        tok.at[pl.ds(near_pair, 2)], x.at[:, quarter(own_quarter)], f_send.at[4], f_recv.at[4], other_core
    ).start()

    def turn_columns(layer, t):
        loads[layer * 4 + t].wait()
        wq_t[layer, t] = wq_in[layer, t].T

    def turn_out(layer):
        loads[layer * 4 + 3].wait()
        for m in range(3):
            wo_t[layer, m * 256 : (m + 1) * 256] = wo_in[layer, :, m * 256 : (m + 1) * 256].T
        row = gain[layer : layer + 1, :].astype(f32)
        gain_t[layer] = jnp.broadcast_to(row, (128, D)).T

    clock = Clock()

    def project(layer, t, b):
        for s in range(2):
            columns = jnp.dot(wq_t[layer, t], x[s, :, block(b)], preferred_element_type=f32)
            qkv[layer, t, :, s * HEAD_DIM : (s + 1) * HEAD_DIM, block(b)] = columns.astype(bf16).reshape(
                CORE_HEADS, HEAD_DIM, BLOCK
            )
        clock.spend(0.5)

    turn_columns(0, 0)
    turn_columns(0, 1)
    for k, (b, s) in enumerate(pieces):
        arrived = piece(far_quarter, b, s)
        remote(arrived, arrived, x_send.at[k], x_recv.at[k], partner).wait_recv()
        remote(arrived, arrived, f_send.at[k], f_recv.at[k], other_core).start()
        if k == 0:
            turn_columns(0, 2)
            own_tokens.wait()
            near = x.at[:, quarter(2 * xl + 1 - core)]
            remote(near, near, f_send.at[4], f_recv.at[4], other_core).wait_recv()
        if k == 2:
            for j in range(2):
                arrived = piece(2 * (1 - xl) + 1 - core, *pieces[j])
                remote(arrived, arrived, f_send.at[j], f_recv.at[j], other_core).wait_recv()
            project(0, 0, 0)
            project(0, 1, 0)
    for j in range(2, 4):
        arrived = piece(2 * (1 - xl) + 1 - core, *pieces[j])
        remote(arrived, arrived, f_send.at[j], f_recv.at[j], other_core).wait_recv()
    project(0, 1, 1)

    def tokens_sent():
        for k, (b, s) in enumerate(pieces):
            arrived = piece(far_quarter, b, s)
            remote(arrived, arrived, x_send.at[k], x_recv.at[k], partner).wait_send()
            remote(arrived, arrived, f_send.at[k], f_recv.at[k], other_core).wait_send()
        near = x.at[:, quarter(own_quarter)]
        remote(near, near, f_send.at[4], f_recv.at[4], other_core).wait_send()

    plane_pos = xpos * (NY // 2) + lax.div(y, 2)
    z_pos = lax.div(z, 2)
    plane_parity, z_parity = lax.rem(xpos + y, 2), lax.rem(z, 2)

    def taker(table):
        taken = [0]

        def take(count):
            first = taken[0]
            taken[0] += count
            return lambda i: table.at[first + i]

        return take

    row = RES * 4

    def colour_rings(b):
        take_ring, take_direct = taker(ring_sems.at[b]), taker(direct_sems.at[b])

        def ring(axis, rows, width, kind=Ring):
            n, pos, right, left = {
                "x": (NX, xpos, x_right, x_left),
                "y": (NY, y, y_right, y_left),
                "z": (NZ, z, z_right, z_left),
            }[axis]
            count = 2 * (n - 1) * (2 if kind is CodedRing else 1)
            return kind(clock, axis, rows * row * width, n, pos, right, left, take_ring(count), take_ring(count))

        def direct(peers, width):
            pos, parity = (plane_pos, plane_parity) if peers is plane else (z_pos, z_parity)
            return Direct(
                clock, 8 * row * width, peers, pos, parity == b, take_direct(len(peers)), take_direct(len(peers))
            )

        return [
            dict(
                down=[ring("z", 32, 0.5, CodedRing)], owners=direct(plane, 1), spread=direct(plane, 0.5), up=[ring("z", 32, 0.5)]
            )
        ] + [
            dict(
                down=[ring(first, 64, 0.5, CodedRing), ring(second, 16, 1)],
                owners=direct(along_z, 1),
                spread=direct(along_z, 0.5),
                up=[ring(second, 16, 0.5), ring(first, 64, 0.5)],
            )
            for first, second in (("y", "x"), ("x", "y"))
        ]

    groups = [colour_rings(b) for b in range(2)]

    def slots(ref, b):
        return lambda i: ref.at[b, i]

    def pairs(ref, b):
        return lambda owner, half: ref.at[b, 2 * owner + half]

    def fours(ref, b):
        return lambda owner, half: ref.at[b, owner, pl.ds(4 * half, 4)]

    def coded(codes, units, b):
        return lambda i: (codes.at[b, i], units.at[b, i])

    def terms(view):
        return lambda owner, half: view(owner, half)[...].reshape(-1, RES)

    places = [
        dict(s=s_a, r=(r_a, ur_a), e=(e_a, ue_a), r2=None, acc=None, last=acc_a, d=d_a, w=w_a, g=g_a, view=pairs, blocks=(8, 32)),
        dict(s=s_b, r=(r_b, ur_b), e=(e_b, ue_b), r2=r_b2, acc=acc_b, last=acc_b2, d=d_b, w=w_b, g=g_b, view=fours, blocks=(2, 8, 16)),
        dict(s=s_c, r=(r_c, ur_c), e=(e_c, ue_c), r2=r_c2, acc=acc_c, last=acc_c2, d=d_c, w=w_c, g=g_c, view=fours, blocks=(2, 8, 16)),
    ]
    middle = [None, lambda b: lambda owner, half: w_b.at[b, y, 2 * owner + half],
              lambda b: lambda owner, half: w_c.at[b, xpos, 2 * owner + half]]

    def trade(layer, b, colour, owner):
        part = att.at[layer, :, owner, pl.ds(128 * colour, 128), block(b)]
        return remote(part, part, t_send.at[b, colour], t_recv.at[layer, b, colour], other_core)

    def score(layer, b, colour):
        place = places[colour]
        blocks = place["blocks"]

        def body(h, carry):
            head = 2 * colour + h
            scores = jnp.dot(
                qkv[layer, 0, head, :, block(b)].T, qkv[layer, 1, head], preferred_element_type=f32
            )
            place["s"][b, pl.ds(h * blocks[0], blocks[0])] = scores.reshape(*blocks, RES)
            return carry

        lax.fori_loop(0, 2, body, 0)
        clock.spend(0.5)

    def attend(layer, b, colour):
        place = places[colour]
        blocks = place["blocks"]

        def body(h, carry):
            head = 2 * colour + h
            weights = place["w"][b, pl.ds(h * blocks[0], blocks[0])].reshape(BLOCK, RES)
            heads = lax.dot_general(
                qkv[layer, 2, head], weights, (((1,), (1,)), ((), ())), preferred_element_type=f32
            ).astype(bf16)
            at = pl.ds(pl.multiple_of(head * HEAD_DIM, HEAD_DIM), HEAD_DIM)
            for s in range(2):
                att[layer, s, core, at, block(b)] = heads[s * HEAD_DIM : (s + 1) * HEAD_DIM]
            return carry

        lax.fori_loop(0, 2, body, 0)
        clock.spend(0.6)

    def joined(ref, b, first, blocks):
        return ref[b, first : first + blocks].astype(f32).reshape(blocks * 8, RES).astype(bf16)

    def colour_steps(layer, b, colour, done):
        place, group = places[colour], groups[b][colour]
        view, slot, staged = terms(place["view"](place["s"], b)), coded(*place["r"], b), coded(*place["e"], b)
        score(layer, b, colour)
        down = group["down"]
        yield from down[0].scatter(view, slot, staged)
        last = place["last"].at[b]
        if colour == 0:
            for half in range(2):
                last[4 * half : 4 * half + 4] = down[0].scatter_result(view, slot, half).reshape(4, 8, RES)
        else:
            view2, slot2 = pairs(place["acc"], b), slots(place["r2"], b)
            for half in range(2):
                place["acc"][b, 4 * half : 4 * half + 4] = down[0].scatter_result(view, slot, half).reshape(4, 16, RES)
            yield from down[1].scatter(view2, slot2)
            for half in range(2):
                last[2 * half : 2 * half + 2] = down[1].scatter_result(view2, slot2, half).reshape(2, 8, RES)
            down[1].scatter_sent(slot2)
        down[0].scatter_sent(slot)
        yield group["owners"].scatter_start(last, slots(place["d"], b))
        yield group["owners"].turn(last, slots(place["d"], b), group["spread"], place["g"].at[b], scale)
        group["spread"].arrived(place["g"].at[b])
        w, up = place["w"], group["up"]
        if colour == 0:
            for half in range(2):
                w[b, 2 * z + half] = joined(place["g"], b, 4 * half, 4)
        else:
            first, second = (y, xpos) if colour == 1 else (xpos, y)
            for half in range(2):
                w[b, first, 2 * second + half] = joined(place["g"], b, 2 * half, 2)
            yield from up[0].gather(middle[colour](b))
        yield from up[-1].gather(place["view"](w, b))
        attend(layer, b, colour)
        trade(layer, b, colour, core).start()
        done()

    def all_sent(b):
        for colour in range(3):
            place, group = places[colour], groups[b][colour]
            group["owners"].scatter_sent(place["last"].at[b])
            group["spread"].gather_sent(place["g"].at[b])
            group["up"][-1].gather_sent(place["view"](place["w"], b))
            if colour:
                group["up"][0].gather_sent(middle[colour](b))

    def finish(layer, b):
        def body(s, carry):
            heads = att[layer, s, :, :, block(b)].reshape(D, BLOCK)
            update = jnp.dot(wo_t[layer], heads, preferred_element_type=f32)
            summed = x[s, :, block(b)].astype(f32) + update
            mean_sq = jnp.mean(summed * summed, axis=0, keepdims=True)
            gains = gain_t[layer]
            normed = summed * lax.rsqrt(mean_sq + EPSILON) * jnp.concatenate([gains, gains], axis=1)
            x[s, :, block(b)] = normed.astype(bf16)
            if layer + 1 == LAYERS:
                far_out(b, s).start()
            return carry

        lax.fori_loop(0, 2, body, 0)
        clock.spend(1.5)

    def far_out(b, s):
        return remote(
            x.at[s, quarter(far_quarter), block(b)], out.at[near_pair + s, :, block(b)],
            o_send.at[b, s], o_recv.at[b, s], partner,
        )

    def own_out(b):
        return pltpu.make_async_copy(
            x.at[:, quarter(own_quarter), block(b)], out.at[pl.ds(near_pair, 2), :, block(b)], o_local.at[b]
        )

    def finish_steps(layer, b):
        yield clock.now + ((2.4, 2.4)[layer] if b == 0 else 1.6)
        for colour in range(3):
            trade(layer, b, colour, 1 - core).wait_recv()
        finish(layer, b)
        if layer + 1 < LAYERS:
            if b == 0:
                project(layer + 1, 0, b)
            project(layer + 1, 1, b)
        else:
            own_out(b).start()

    for layer in range(LAYERS):
        running, order = [], [0]

        def add(steps, running=running, order=order):
            due = next(steps, None)
            if due is not None:
                order[0] += 1
                running.append((due, order[0], steps))

        def launch(b, colour, layer=layer, add=add):
            left[b][colour] = 1

            def done():
                left[b][colour] = 0
                if sum(left[b].values()) == 0 and len(left[b]) == 3:
                    add(finish_steps(layer, b))

            add(colour_steps(layer, b, colour, done))

        left = [{}, {}]
        for colour in range(3):
            launch(0, colour)
        project(layer, 0, 1)
        for colour in range(3):
            launch(1, colour)
        for b in range(2):
            project(layer, 2, b)
        fillers = []
        if layer == 0:
            tokens_sent()
            fillers = [functools.partial(turn_out, 0)]
            fillers += [functools.partial(turn_columns, 1, t) for t in range(3)]
            fillers += [functools.partial(turn_out, 1)]
        while running:
            running.sort(key=lambda entry: entry[:2])
            if fillers and running[0][0] > clock.now + 0.7:
                fillers.pop(0)()
                clock.spend(1.0)
                continue
            due, _, steps = running.pop(0)
            clock.now = max(clock.now, due)
            add(steps)
        for filler in fillers:
            filler()
        for b in range(2):
            all_sent(b)
            for colour in range(3):
                trade(layer, b, colour, core).wait_send()

    for b in range(2):
        own_out(b).wait()
        for s in range(2):
            far_out(b, s).wait_send()
            landed = out.at[far_pair + s, :, block(b)]
            remote(landed, landed, o_send.at[b, s], o_recv.at[b, s], partner).wait_recv()


def on_device(tokens, qkv_weight, out_weight, norm_gain):
    scale = 1.0 / (HEAD_DIM * 2 * NX * NY * NZ) ** 0.5
    any_space = pl.BlockSpec(memory_space=pl.ANY)
    vmem = pl.BlockSpec(memory_space=pltpu.VMEM)
    dma = pltpu.SemaphoreType.DMA
    around = lambda n: 2 * (n - 1)
    ring_count = 4 * (around(NZ) + 2 * around(NX) + 2 * around(NY)) + 2 * (around(NZ) + around(NX) + around(NY))
    direct_count = 4 * (NX * NY - 1 + 2 * (NZ - 1))
    result = pl.pallas_call(
        functools.partial(whole, scale),
        out_shape=jax.ShapeDtypeStruct((4, QUARTER, RES), bf16),
        in_specs=[any_space, any_space, any_space, vmem],
        out_specs=any_space,
        scratch_shapes=[
            pltpu.VMEM((2, D, RES), bf16),
            pltpu.VMEM((LAYERS, 3, D, CORE_COLS), bf16),
            pltpu.VMEM((LAYERS, D, D), bf16),
            pltpu.VMEM((LAYERS, 3, CORE_COLS, D), bf16),
            pltpu.VMEM((LAYERS, D, D), bf16),
            pltpu.VMEM((LAYERS, D, 128), f32),
            pltpu.VMEM((LAYERS, 3, CORE_HEADS, 2 * HEAD_DIM, RES), bf16),
            pltpu.VMEM((LAYERS, 2, 2, CORE_COLS, RES), bf16),
            pltpu.VMEM((2, 16, 32, RES), f32),
            pltpu.VMEM((2, 4, 8, 16, RES), f32),
            pltpu.VMEM((2, 4, 8, 16, RES), f32),
            pltpu.VMEM((2, 14, 32, RES), bf16),
            pltpu.VMEM((2, 6, 64, RES), bf16),
            pltpu.VMEM((2, 6, 64, RES), bf16),
            pltpu.VMEM((2, 8, 8, RES), f32),
            pltpu.VMEM((2, 8, 16, RES), f32),
            pltpu.VMEM((2, 8, 16, RES), f32),
            pltpu.VMEM((2, 6, 16, RES), f32),
            pltpu.VMEM((2, 6, 16, RES), f32),
            pltpu.VMEM((2, 4, 8, RES), f32),
            pltpu.VMEM((2, 4, 8, RES), f32),
            pltpu.VMEM((2, 15, 8, RES), f32),
            pltpu.VMEM((2, 7, 8, RES), f32),
            pltpu.VMEM((2, 7, 8, RES), f32),
            pltpu.VMEM((2, 16, 32, RES), bf16),
            pltpu.VMEM((2, 4, 8, 16, RES), bf16),
            pltpu.VMEM((2, 4, 8, 16, RES), bf16),
            pltpu.VMEM((2, 8, 8, RES), bf16),
            pltpu.VMEM((2, 4, 8, RES), bf16),
            pltpu.VMEM((2, 4, 8, RES), bf16),
            pltpu.VMEM((2, 4, 32, RES), bf16),
            pltpu.VMEM((2, 4, 64, RES), bf16),
            pltpu.VMEM((2, 4, 64, RES), bf16),
            pltpu.VMEM((2, 4, 8, 128), f32),
            pltpu.VMEM((2, 4, 8, 128), f32),
            pltpu.VMEM((2, 4, 8, 128), f32),
            pltpu.VMEM((2, 14, 8, 128), f32),
            pltpu.VMEM((2, 6, 8, 128), f32),
            pltpu.VMEM((2, 6, 8, 128), f32),
            dma((2, ring_count)),
            dma((2, direct_count)),
            dma((4 * LAYERS,)),
            dma,
            dma((4,)),
            dma((4,)),
            dma((5,)),
            dma((5,)),
            dma((2, 3)),
            dma((LAYERS, 2, 3)),
            dma((2,)),
            dma((2, 2)),
            dma((2, 2)),
        ],
        compiler_params=pltpu.CompilerParams(
            collective_id=0, has_side_effects=True, vmem_limit_bytes=60 * 1024 * 1024
        ),
    )(
        tokens.transpose(0, 2, 1),
        qkv_weight.transpose(0, 2, 1, 3),
        out_weight,
        norm_gain,
    )
    return result.transpose(0, 2, 1)


def solution(mesh):
    finer = Mesh(mesh.devices.reshape(NY, NX // 2, NZ, 2, 2), AXES)
    rows, heads = ("y", "xh", "z"), ("xl", "core")
    return jax.shard_map(
        on_device,
        mesh=finer,
        in_specs=(P(rows, None, heads), P(), P(), P()),
        out_specs=P(rows, None, heads),
        check_vma=False,
    )
```
